256 devices in a mesh: section: 4 (over x), expert: 32 (over z, y_lo, core), dp: 2 (over y_hi).
Axes of the slice: x: 4, y: 4 (y_hi: 2, y_lo: 2; y = y_hi * 2 + y_lo), z: 8, core: 2. Of those that a mesh axis runs over, the one named last changes fastest.
Arguments:
- fwd_in: bfloat16 [4, 3072, 2048], P('section', 'expert'), may hold values from -6 to 6
- fwd_routes: int32 [4, 3072, 8], P('section', 'expert'), may hold values from 0 to 31, all different within a row; in each aligned block of 96 rows (0 to 95, 96 to 191, ..., all dimensions but the last counted through in order) at most 26 rows name the same one
- fwd_numer: int32 [4, 3072, 8], P('section', 'expert'), may hold values from 1 to 255
- bwd_saved: bfloat16 [4, 3072, 2048], P('section', 'expert'), may hold values from -6 to 6
- bwd_routes: int32 [4, 3072, 8], P('section', 'expert'), may hold values from 0 to 31, all different within a row; in each aligned block of 96 rows (0 to 95, 96 to 191, ..., all dimensions but the last counted through in order) at most 26 rows name the same one
- bwd_numer: int32 [4, 3072, 8], P('section', 'expert'), may hold values from 1 to 255
- bwd_grad: bfloat16 [4, 3072, 2048], P('section', 'expert'), may hold values from -6 to 6
- w_gate: bfloat16 [4, 32, 2048, 768], P('section', 'expert', None, 'dp'), may hold values from -0.125 to 0.125
- w_up: bfloat16 [4, 32, 2048, 768], P('section', 'expert', None, 'dp'), may hold values from -0.125 to 0.125
- w_down: bfloat16 [4, 32, 768, 2048], P('section', 'expert', 'dp'), may hold values from -0.21875 to 0.21875
Outputs:
- next_fwd: bfloat16 [4, 3072, 2048], P('section', 'expert')
- next_bwd: bfloat16 [4, 3072, 2048], P('section', 'expert')
- grad_gate: bfloat16 [4, 32, 2048, 768], P('section', 'expert', None, 'dp')
- grad_up: bfloat16 [4, 32, 2048, 768], P('section', 'expert', None, 'dp')
- grad_down: bfloat16 [4, 32, 768, 2048], P('section', 'expert', 'dp')
The draws below stay inside these ranges and needn't reach their ends.
Inputs may be any that keep to these rules, and one draw needn't show every extreme that they name: `fwd_routes`: each token names 8 different experts. In each aligned block of 96 rows (the tokens of one index of expert of one section) no expert is named more than 26 times; in some blocks some expert is named exactly 26 times. `bwd_routes`: each token names 8 different experts. In each aligned block of 96 rows (the tokens of one index of expert of one section) no expert is named more than 26 times; in some blocks some expert is named exactly 26 times.
All inputs are finite; a program needn't handle non-finite values.
Results may differ from the reference program's by a relative error of at most 0.0058.
Values may be sent and summed in bfloat16 or wider, within the bound.
A program may use at most 128 MiB of HBM per device.

```python
import math
import jax
import jax.numpy as jnp
import numpy as np
from jax import lax

D = 2048
FF = 768
TOP = 8
EXPERTS = 32
TOK_DEV = 96
MOST = 26
TOKENS = 3072
N_SECTION = 4


def place_ends(entries, own_key, low, high):
    longest = entries.shape.index(max(entries.shape))
    spots = []
    for shift in (0, 1):
        where = [jax.random.randint(jax.random.fold_in(own_key, axis), (), 0, length) for axis, length in enumerate(entries.shape)]
        where[longest] = (where[longest] + shift) % entries.shape[longest]
        spots.append(tuple(where))
    return entries.at[spots[0]].set(low).at[spots[1]].set(high)


def shard_levels(key, dims, pieces, smallest, largest):
    def one(position, shards_of):
        draws = jax.random.uniform(jax.random.fold_in(jax.random.fold_in(key, 6), position), (shards_of,), jnp.float32, smallest / len(pieces), largest / len(pieces))
        return jnp.repeat(jnp.exp(draws), dims[position] // shards_of).reshape((-1,) + (1,) * (len(dims) - position - 1))

    gain = one(*pieces[0])
    for cut in pieces[1:]:
        gain = gain * one(*cut)
    return gain


def shared_out(stream_key, own, number, rows, number_of, top, limit, slope):
    ranking = jax.random.permutation(stream_key, number_of)
    heavy_load, usual = portions_of(number_of, rows * top, limit, slope, True), portions_of(number_of, rows * top, limit, slope, False)
    places = jnp.arange(number_of)

    def named(sizes, offset_by):
        used = int((sizes > 0).sum())
        fixed = max(1, used // 4)
        moved = fixed + (places - fixed + offset_by * (used - fixed)) % max(1, number_of - fixed)
        return jnp.zeros((number_of,), jnp.int32).at[ranking[jnp.where(places < fixed, places, moved)]].set(jnp.asarray(sizes, jnp.int32))

    sizes = jnp.where(number % 4 == 0, named(heavy_load, number // 4), named(usual, number - number // 4 - 1))
    mixed = jax.random.permutation(jax.random.fold_in(own, 3), number_of)
    giver, sink = mixed[0:number_of // 2 * 2:2], mixed[1:number_of // 2 * 2:2]
    room = jnp.minimum(sizes[giver] - 1, limit - sizes[sink]) // 2
    room = jnp.where((giver == ranking[0]) | (sink == ranking[0]) | (sizes[sink] == 0), 0, jnp.maximum(room, 0))
    moved = jax.random.randint(jax.random.fold_in(own, 4), (number_of // 2,), 0, 1 << 20) % (room + 1)
    sizes = sizes.at[giver].add(-moved).at[sink].add(moved)
    members = jnp.searchsorted(jnp.cumsum(sizes), jnp.arange(rows * top), side="right").astype(jnp.int32)
    grid = members.reshape(top, rows).T
    grid = grid[jax.random.permutation(jax.random.fold_in(own, 1), rows)]
    offset_by = jax.random.randint(jax.random.fold_in(own, 2), (rows, 1), 0, top)
    return jnp.take_along_axis(grid, (jnp.arange(top)[None, :] + offset_by) % top, axis=1)


def portions_of(count, total, bound, slope, full):
    loads = [(1 << 20) // math.isqrt(grade ** slope) + 1 for grade in range(1, count + 1)]
    largest = bound if full else min(bound, max(-(-total // count), total * loads[0] // sum(loads)))
    least = 1 if total - largest >= count - 1 else 0
    given, rest = [largest] + [least] * (count - 1), total - largest - least * (count - 1)
    while rest > 0:
        movable = [i for i in range(1, count) if given[i] < largest] or [i for i in range(1, count) if given[i] < bound]
        whole, left = sum([loads[i] for i in movable]), rest
        for i in movable:
            more = min(bound - given[i], max(1, left * loads[i] // whole), rest)
            given[i] = given[i] + more
            rest = rest - more
    return np.array(given)


def centred(own_key, shape, deviation, reach, shards=(), held_as=jnp.bfloat16):
    loudness = shard_levels(own_key, shape, shards, -0.22, 0.18) if shards else 1.0
    values = jax.random.normal(own_key, shape, jnp.float32) * deviation * loudness
    return jnp.minimum(jnp.maximum(values, -reach), reach).astype(held_as)


def setup_inputs(seed: int = 0) -> dict:
    key_of = jax.random.split(jax.random.key(seed), 11)
    fwd_in = centred(key_of[0], (N_SECTION, TOKENS, D), 1.0, 6.0, ((0, 4), (1, 32)))
    fwd_routes_keys = jax.random.split(jax.random.fold_in(key_of[1], 1), N_SECTION * TOKENS // TOK_DEV)
    fwd_routes_turns = jax.random.permutation(jax.random.fold_in(key_of[1], 3), N_SECTION * TOKENS // TOK_DEV)
    fwd_routes = jax.vmap(lambda own, number: shared_out(jax.random.fold_in(key_of[1], 2), own, number, TOK_DEV, EXPERTS, TOP, MOST, 2))(fwd_routes_keys, fwd_routes_turns).reshape((N_SECTION, TOKENS, TOP))
    fwd_numer = place_ends(jax.random.randint(key_of[2], (N_SECTION, TOKENS, TOP), 1, 256), jax.random.fold_in(key_of[2], 1), 1, 255).astype(jnp.int32)
    bwd_saved = centred(key_of[3], (N_SECTION, TOKENS, D), 1.0, 6.0, ((0, 4), (1, 32)))
    bwd_routes_keys = jax.random.split(jax.random.fold_in(key_of[4], 1), N_SECTION * TOKENS // TOK_DEV)
    bwd_routes_turns = jax.random.permutation(jax.random.fold_in(key_of[4], 3), N_SECTION * TOKENS // TOK_DEV)
    bwd_routes = jax.vmap(lambda own, number: shared_out(jax.random.fold_in(key_of[4], 2), own, number, TOK_DEV, EXPERTS, TOP, MOST, 2))(bwd_routes_keys, bwd_routes_turns).reshape((N_SECTION, TOKENS, TOP))
    bwd_numer = place_ends(jax.random.randint(key_of[5], (N_SECTION, TOKENS, TOP), 1, 256), jax.random.fold_in(key_of[5], 1), 1, 255).astype(jnp.int32)
    bwd_grad = centred(key_of[6], (N_SECTION, TOKENS, D), 1.0, 6.0, ((0, 4), (1, 32)))
    w_gate = centred(key_of[7], (N_SECTION, EXPERTS, D, FF), D ** -0.5, 0.125, ((0, 4), (1, 32), (3, 2)))
    w_up = centred(key_of[8], (N_SECTION, EXPERTS, D, FF), D ** -0.5, 0.125, ((0, 4), (1, 32), (3, 2)))
    w_down = centred(key_of[9], (N_SECTION, EXPERTS, FF, D), FF ** -0.5, 0.21875, ((0, 4), (1, 32), (2, 2)))
    return {"fwd_in": fwd_in, "fwd_routes": fwd_routes, "fwd_numer": fwd_numer, "bwd_saved": bwd_saved, "bwd_routes": bwd_routes, "bwd_numer": bwd_numer, "bwd_grad": bwd_grad, "w_gate": w_gate, "w_up": w_up, "w_down": w_down}


def slot_positions(routes, capacity):
    flat_routes = routes.reshape(-1)
    onehot_table = (flat_routes[:, None] == jnp.arange(EXPERTS, dtype=jnp.int32)[None, :]).astype(jnp.int32)
    earlier = jnp.cumsum(onehot_table, 0) - onehot_table
    return (flat_routes * capacity + jnp.sum(earlier * onehot_table, 1)).astype(jnp.int32)


def combine_weights(numerators):
    counted = numerators.astype(jnp.float32)
    return counted / jnp.sum(counted, -1, keepdims=True)


def expert_buffer(rows, positions, capacity):
    filled = jnp.zeros((EXPERTS * capacity, rows.shape[-1]), rows.dtype).at[positions].set(rows)
    return filled.reshape(EXPERTS, capacity, rows.shape[-1])


def forward_expert(operands):
    rows, gate_weight, up_weight, down_weight = operands
    gate_value = jnp.dot(rows, gate_weight, preferred_element_type=jnp.float32)
    up_value = jnp.dot(rows, up_weight, preferred_element_type=jnp.float32)
    hidden = (jax.nn.silu(gate_value) * up_value).astype(jnp.bfloat16)
    return jnp.dot(hidden, down_weight, preferred_element_type=jnp.float32).astype(jnp.bfloat16)


def backward_expert(operands):
    rows, grad_rows, gate_weight, up_weight, down_weight = operands
    gate_value = jnp.dot(rows, gate_weight, preferred_element_type=jnp.float32)
    up_value = jnp.dot(rows, up_weight, preferred_element_type=jnp.float32)
    silu_gate = jax.nn.silu(gate_value)
    sigmoid_gate = jax.nn.sigmoid(gate_value)
    hidden = (silu_gate * up_value).astype(jnp.bfloat16)
    hidden_grad = jnp.dot(grad_rows, down_weight.T, preferred_element_type=jnp.float32)
    up_grad = (hidden_grad * silu_gate).astype(jnp.bfloat16)
    gate_grad = (hidden_grad * up_value * sigmoid_gate * (1.0 + gate_value * (1.0 - sigmoid_gate))).astype(jnp.bfloat16)
    row_grad = (jnp.dot(gate_grad, gate_weight.T, preferred_element_type=jnp.float32)
                + jnp.dot(up_grad, up_weight.T, preferred_element_type=jnp.float32)).astype(jnp.bfloat16)
    down_sum = jnp.dot(hidden.T, grad_rows, preferred_element_type=jnp.float32).astype(jnp.bfloat16)
    gate_sum = jnp.dot(rows.T, gate_grad, preferred_element_type=jnp.float32).astype(jnp.bfloat16)
    up_sum = jnp.dot(rows.T, up_grad, preferred_element_type=jnp.float32).astype(jnp.bfloat16)
    return row_grad, gate_sum, up_sum, down_sum


def reference(fwd_in, fwd_routes, fwd_numer, bwd_saved, bwd_routes, bwd_numer, bwd_grad, w_gate, w_up, w_down):
    capacity = TOKENS // TOK_DEV * MOST
    outputs_list = []
    inputs_grads = []
    gate_grads = []
    up_grads = []
    down_grads = []
    for section_idx in range(N_SECTION):
        inputs = fwd_in[section_idx]
        positions = slot_positions(fwd_routes[section_idx], capacity)
        rows = expert_buffer(jnp.repeat(inputs, TOP, 0), positions, capacity)
        expert_out = lax.map(forward_expert, (rows, w_gate[section_idx], w_up[section_idx], w_down[section_idx]))
        picked = expert_out.reshape(-1, D)[positions].reshape(TOKENS, TOP, D).astype(jnp.float32)
        mixing = combine_weights(fwd_numer[section_idx])
        layer_out = (inputs.astype(jnp.float32) + jnp.sum(mixing[:, :, None] * picked, 1)).astype(jnp.bfloat16)
        outputs_list.append(layer_out)

        saved = bwd_saved[section_idx]
        grad_in = bwd_grad[section_idx]
        back_positions = slot_positions(bwd_routes[section_idx], capacity)
        back_mixing = combine_weights(bwd_numer[section_idx])
        scaled_grad = (back_mixing[:, :, None] * grad_in.astype(jnp.float32)[:, None, :]).astype(jnp.bfloat16)
        saved_rows = expert_buffer(jnp.repeat(saved, TOP, 0), back_positions, capacity)
        grad_rows = expert_buffer(scaled_grad.reshape(-1, D), back_positions, capacity)
        row_grad, gate_sum, up_sum, down_sum = lax.map(
            backward_expert, (saved_rows, grad_rows, w_gate[section_idx], w_up[section_idx], w_down[section_idx]))
        picked_grad = row_grad.reshape(-1, D)[back_positions].reshape(TOKENS, TOP, D).astype(jnp.float32)
        input_grad = (grad_in.astype(jnp.float32) + jnp.sum(picked_grad, 1)).astype(jnp.bfloat16)
        inputs_grads.append(input_grad)
        gate_grads.append(gate_sum)
        up_grads.append(up_sum)
        down_grads.append(down_sum)
    next_fwd = jnp.roll(jnp.stack(outputs_list), 1, 0)
    next_bwd = jnp.roll(jnp.stack(inputs_grads), -1, 0)
    return next_fwd, next_bwd, jnp.stack(gate_grads), jnp.stack(up_grads), jnp.stack(down_grads)
```

```python
import jax
import jax.numpy as jnp
from jax import lax
from jax.sharding import PartitionSpec as P

EXPERTS = 32
MOST = 26


def passed_along(block, axis, distance):
    devices = range(lax.axis_size(axis))
    route = [((i - distance) % len(devices), i) for i in devices]
    return lax.ppermute(block, axis, route)


def swapped(block):
    return lax.ppermute(block, "dp", [(0, 1), (1, 0)])


def slot_ranks(routes):
    flat_routes = routes.reshape(-1)
    onehot_table = (flat_routes[:, None] == jnp.arange(EXPERTS, dtype=jnp.int32)[None, :]).astype(
        jnp.int32
    )
    earlier = jnp.cumsum(onehot_table, 0) - onehot_table
    return (flat_routes, jnp.sum(earlier * onehot_table, 1))


def combine_weights(numerators):
    counted = numerators.astype(jnp.float32)
    return counted / jnp.sum(counted, -1, keepdims=True)


def packed_rows(rows, positions, groups):
    filled = jnp.zeros((EXPERTS * MOST, rows.shape[-1]), rows.dtype).at[positions].set(rows)
    return filled.reshape(groups, EXPERTS // groups, MOST, rows.shape[-1])


def handoff(value, direction):
    return passed_along(value, "section", direction)


def project(rows, gate_weight, up_weight):
    gate_value = jnp.einsum("semd,edf->semf", rows, gate_weight, preferred_element_type=jnp.float32)
    up_value = jnp.einsum("semd,edf->semf", rows, up_weight, preferred_element_type=jnp.float32)
    return (gate_value, up_value)


def local_backward(gate_value, up_value, grad_rows, down_weight):
    silu_gate = jax.nn.silu(gate_value)
    sigmoid_gate = jax.nn.sigmoid(gate_value)
    hidden = (silu_gate * up_value).astype(jnp.bfloat16)
    hidden_grad = jnp.einsum(
        "semd,efd->semf", grad_rows, down_weight, preferred_element_type=jnp.float32
    )
    up_grad = (hidden_grad * silu_gate).astype(jnp.bfloat16)
    gate_grad = (
        hidden_grad * up_value * sigmoid_gate * (1.0 + gate_value * (1.0 - sigmoid_gate))
    ).astype(jnp.bfloat16)
    return (hidden, gate_grad, up_grad)


def weight_terms(saved_rows, grad_rows, back_hidden, gate_grad, up_grad):
    gate_term = jnp.einsum(
        "semd,semf->edf", saved_rows, gate_grad, preferred_element_type=jnp.float32
    )
    up_term = jnp.einsum("semd,semf->edf", saved_rows, up_grad, preferred_element_type=jnp.float32)
    down_term = jnp.einsum(
        "semf,semd->efd", back_hidden, grad_rows, preferred_element_type=jnp.float32
    )
    return (gate_term, up_term, down_term)


def mix_rows(base, returned, positions, weights, choices_per):
    width = returned.shape[-1]
    picked = (
        returned.reshape(-1, width)[positions].reshape(-1, choices_per, width).astype(jnp.float32)
    )
    return (base.astype(jnp.float32) + jnp.sum(weights[:, :, None] * picked, 1)).astype(
        jnp.bfloat16
    )


def local(
    fwd_in, fwd_routes, fwd_numer, bwd_saved, bwd_routes, bwd_numer, bwd_grad, w_gate, w_up, w_down
):
    groups = lax.axis_size("expert")
    inputs = fwd_in[0]
    saved = bwd_saved[0]
    grad_in = bwd_grad[0]
    model_width = inputs.shape[-1]
    half = model_width // lax.axis_size("dp")
    mine = lax.axis_index("dp") * half
    theirs = half - mine
    choices_per = fwd_routes.shape[-1]
    gate_half = w_gate[0]
    up_half = w_up[0]
    down_half = w_down[0]
    down_recv, gate_recv, up_recv = swapped(
        (
            lax.dynamic_slice_in_dim(down_half, theirs, half, 2),
            lax.dynamic_slice_in_dim(gate_half, theirs, half, 1),
            lax.dynamic_slice_in_dim(up_half, theirs, half, 1),
        )
    )
    down_mine = jnp.concatenate([lax.dynamic_slice_in_dim(down_half, mine, half, 2), down_recv], 1)
    gate_mine = jnp.concatenate([lax.dynamic_slice_in_dim(gate_half, mine, half, 1), gate_recv], 2)
    up_mine = jnp.concatenate([lax.dynamic_slice_in_dim(up_half, mine, half, 1), up_recv], 2)

    fwd_flat, fwd_rank = slot_ranks(fwd_routes[0])
    back_flat, back_rank = slot_ranks(bwd_routes[0])
    fwd_positions = fwd_flat * MOST + fwd_rank
    back_positions = back_flat * MOST + back_rank
    mixing = combine_weights(fwd_numer[0])
    back_mixing = combine_weights(bwd_numer[0])
    unit_weights = jnp.ones_like(back_mixing)
    scaled_grad = (back_mixing[:, :, None] * grad_in.astype(jnp.float32)[:, None, :]).astype(
        jnp.bfloat16
    )
    send_inputs = packed_rows(jnp.repeat(inputs, choices_per, 0), fwd_positions, groups)
    send_saved = packed_rows(jnp.repeat(saved, choices_per, 0), back_positions, groups)
    send_grad = packed_rows(scaled_grad.reshape(-1, model_width), back_positions, groups)
    recv_inputs = lax.all_to_all(send_inputs, "expert", split_axis=0, concat_axis=0, tiled=True)
    recv_saved = lax.all_to_all(send_saved, "expert", split_axis=0, concat_axis=0, tiled=True)
    recv_grad = lax.all_to_all(send_grad, "expert", split_axis=0, concat_axis=0, tiled=True)

    gate_value, up_value = project(recv_inputs, gate_half, up_half)
    hidden = (jax.nn.silu(gate_value) * up_value).astype(jnp.bfloat16)
    hidden_all = jnp.concatenate([hidden, swapped(hidden)], -1)
    out_part = jnp.einsum(
        "semf,efd->semd", hidden_all, down_mine, preferred_element_type=jnp.float32
    ).astype(jnp.bfloat16)

    back_gate, back_up = project(recv_saved, gate_half, up_half)
    back_hidden, gate_grad, up_grad = local_backward(back_gate, back_up, recv_grad, down_half)
    gate_term, up_term, down_term = weight_terms(
        recv_saved, recv_grad, back_hidden, gate_grad, up_grad
    )
    gate_other, up_other = swapped((gate_grad, up_grad))
    gate_all = jnp.concatenate([gate_grad, gate_other], -1)
    up_all = jnp.concatenate([up_grad, up_other], -1)
    grad_part = (
        jnp.einsum("semf,edf->semd", gate_all, gate_mine, preferred_element_type=jnp.float32)
        + jnp.einsum("semf,edf->semd", up_all, up_mine, preferred_element_type=jnp.float32)
    ).astype(jnp.bfloat16)

    back_out = lax.all_to_all(out_part, "expert", split_axis=0, concat_axis=0, tiled=True)
    back_grad = lax.all_to_all(grad_part, "expert", split_axis=0, concat_axis=0, tiled=True)
    inputs_part = lax.dynamic_slice_in_dim(inputs, mine, half, 1)
    grad_in_part = lax.dynamic_slice_in_dim(grad_in, mine, half, 1)
    layer_out = mix_rows(inputs_part, back_out, fwd_positions, mixing, choices_per)
    input_grad = mix_rows(grad_in_part, back_grad, back_positions, unit_weights, choices_per)
    layer_out = lax.all_gather(layer_out, "dp", axis=1, tiled=True)
    input_grad = lax.all_gather(input_grad, "dp", axis=1, tiled=True)
    next_fwd = handoff(layer_out[None], 1)
    next_bwd = handoff(input_grad[None], -1)
    gate_sum = gate_term.astype(jnp.bfloat16)
    up_sum = up_term.astype(jnp.bfloat16)
    down_sum = down_term.astype(jnp.bfloat16)
    return (next_fwd, next_bwd, gate_sum[None], up_sum[None], down_sum[None])


def solution(mesh):
    in_specs = (
        P("section", "expert", None),
        P("section", "expert", None),
        P("section", "expert", None),
        P("section", "expert", None),
        P("section", "expert", None),
        P("section", "expert", None),
        P("section", "expert", None),
        P("section", "expert", None, "dp"),
        P("section", "expert", None, "dp"),
        P("section", "expert", "dp", None),
    )
    out_specs = (
        P("section", "expert", None),
        P("section", "expert", None),
        P("section", "expert", None, "dp"),
        P("section", "expert", None, "dp"),
        P("section", "expert", "dp", None),
    )
    return jax.shard_map(local, mesh=mesh, in_specs=in_specs, out_specs=out_specs, check_vma=False)
```

```python
import functools

import jax
import jax.numpy as jnp
from jax import lax
from jax.experimental import pallas as pl
from jax.experimental.pallas import tpu as pltpu
from jax.sharding import PartitionSpec as P

MESH = pl.DeviceIdType.MESH

EXPERTS = 32
MOST = 26


def passed_along(block, axis, distance):
    devices = range(lax.axis_size(axis))
    route = [((i - distance) % len(devices), i) for i in devices]
    return lax.ppermute(block, axis, route)


def swapped(block):
    return lax.ppermute(block, "dp", [(0, 1), (1, 0)])


def dispatch_kernel(n, *refs):
    sends, swaps_out, recvs, swaps_in = refs[0:3], refs[3:6], refs[6:9], refs[9:12]
    send_sems, recv_sems, w_send, w_recv, local_sems = refs[12:]
    me = lax.axis_index("expert")
    other = 1 - lax.axis_index("dp")

    barrier = pltpu.get_barrier_semaphore()

    def greet(o, carry):
        pl.semaphore_signal(barrier, 1, device_id={"expert": lax.rem(me + o, n)}, device_id_type=MESH)
        return carry

    lax.fori_loop(1, n, greet, 0)
    pl.semaphore_signal(barrier, 1, device_id={"dp": other}, device_id_type=MESH)
    pl.semaphore_wait(barrier, n)

    def copy_of(a, o):
        target = lax.rem(me + o, n)
        return pltpu.make_async_remote_copy(
            src_ref=sends[a].at[target],
            dst_ref=recvs[a].at[me],
            send_sem=send_sems.at[a, o],
            recv_sem=recv_sems.at[a, o],
            device_id={"expert": target},
            device_id_type=MESH,
        )

    swaps = [
        pltpu.make_async_remote_copy(
            src_ref=swaps_out[i],
            dst_ref=swaps_in[i],
            send_sem=w_send.at[i],
            recv_sem=w_recv.at[i],
            device_id={"dp": other},
            device_id_type=MESH,
        )
        for i in range(3)
    ]
    locals_ = [pltpu.make_async_copy(sends[a].at[me], recvs[a].at[me], local_sems.at[a]) for a in range(3)]
    for a in range(3):
        locals_[a].start()

        def start(o, carry, a=a):
            copy_of(a, o).start()
            return carry

        lax.fori_loop(1, n, start, 0)
        if a == 0:
            for swap in swaps:
                swap.start()
    for a in range(3):

        def finish(o, carry, a=a):
            copy_of(a, o).wait()
            return carry

        lax.fori_loop(1, n, finish, 0)
        locals_[a].wait()
    for swap in swaps:
        swap.wait()


def dispatch(sends, swaps_out):
    n = sends[0].shape[0]
    anywhere = pl.BlockSpec(memory_space=pl.ANY)
    shapes = [jax.ShapeDtypeStruct(x.shape, x.dtype) for x in (*sends, *swaps_out)]
    outs = pl.pallas_call(
        functools.partial(dispatch_kernel, n),
        out_shape=shapes,
        in_specs=[anywhere] * 6,
        out_specs=[anywhere] * 6,
        scratch_shapes=[
            pltpu.SemaphoreType.DMA((3, n)),
            pltpu.SemaphoreType.DMA((3, n)),
            pltpu.SemaphoreType.DMA((3,)),
            pltpu.SemaphoreType.DMA((3,)),
            pltpu.SemaphoreType.DMA((3,)),
        ],
        compiler_params=pltpu.CompilerParams(collective_id=0, has_side_effects=True),
    )(*sends, *swaps_out)
    return outs[0:3], outs[3:6]


def slot_ranks(routes):
    flat_routes = routes.reshape(-1)
    onehot_table = (flat_routes[:, None] == jnp.arange(EXPERTS, dtype=jnp.int32)[None, :]).astype(
        jnp.int32
    )
    earlier = jnp.cumsum(onehot_table, 0) - onehot_table
    return (flat_routes, jnp.sum(earlier * onehot_table, 1))


def combine_weights(numerators):
    counted = numerators.astype(jnp.float32)
    return counted / jnp.sum(counted, -1, keepdims=True)


def slot_table(positions, choices_per):
    slots = jnp.arange(EXPERTS * MOST, dtype=jnp.int32)
    return slots[:, None, None] == positions.reshape(-1, choices_per)[None, :, :]


def packed_rows(rows, table, scale=None):
    chosen = jnp.any(table, -1)
    picked = jnp.dot(chosen.astype(rows.dtype), rows, preferred_element_type=jnp.float32)
    if scale is not None:
        picked = picked * jnp.sum(jnp.where(table, scale[None], 0.0), (1, 2))[:, None]
    return picked.astype(rows.dtype).reshape(EXPERTS, MOST, rows.shape[-1])


def handoff(value, direction):
    return passed_along(value, "section", direction)


def project(rows, gate_weight, up_weight):
    gate_value = jnp.einsum("semd,edf->semf", rows, gate_weight, preferred_element_type=jnp.float32)
    up_value = jnp.einsum("semd,edf->semf", rows, up_weight, preferred_element_type=jnp.float32)
    return (gate_value, up_value)


def local_backward(gate_value, up_value, grad_rows, down_weight):
    silu_gate = jax.nn.silu(gate_value)
    sigmoid_gate = jax.nn.sigmoid(gate_value)
    hidden = (silu_gate * up_value).astype(jnp.bfloat16)
    hidden_grad = jnp.einsum(
        "semd,efd->semf", grad_rows, down_weight, preferred_element_type=jnp.float32
    )
    up_grad = (hidden_grad * silu_gate).astype(jnp.bfloat16)
    gate_grad = (
        hidden_grad * up_value * sigmoid_gate * (1.0 + gate_value * (1.0 - sigmoid_gate))
    ).astype(jnp.bfloat16)
    return (hidden, gate_grad, up_grad)


def weight_terms(saved_rows, grad_rows, back_hidden, gate_grad, up_grad):
    gate_term = jnp.einsum(
        "semd,semf->edf", saved_rows, gate_grad, preferred_element_type=jnp.float32
    )
    up_term = jnp.einsum("semd,semf->edf", saved_rows, up_grad, preferred_element_type=jnp.float32)
    down_term = jnp.einsum(
        "semf,semd->efd", back_hidden, grad_rows, preferred_element_type=jnp.float32
    )
    return (gate_term, up_term, down_term)


def mix_rows(base, returned, positions, weights, choices_per):
    width = returned.shape[-1]
    picked = (
        returned.reshape(-1, width)[positions].reshape(-1, choices_per, width).astype(jnp.float32)
    )
    return (base.astype(jnp.float32) + jnp.sum(weights[:, :, None] * picked, 1)).astype(
        jnp.bfloat16
    )


def local(
    fwd_in, fwd_routes, fwd_numer, bwd_saved, bwd_routes, bwd_numer, bwd_grad, w_gate, w_up, w_down
):
    groups = lax.axis_size("expert")
    inputs = fwd_in[0]
    saved = bwd_saved[0]
    grad_in = bwd_grad[0]
    model_width = inputs.shape[-1]
    half = model_width // lax.axis_size("dp")
    mine = lax.axis_index("dp") * half
    theirs = half - mine
    choices_per = fwd_routes.shape[-1]
    gate_half = w_gate[0]
    up_half = w_up[0]
    down_half = w_down[0]

    fwd_flat, fwd_rank = slot_ranks(fwd_routes[0])
    back_flat, back_rank = slot_ranks(bwd_routes[0])
    fwd_positions = fwd_flat * MOST + fwd_rank
    back_positions = back_flat * MOST + back_rank
    mixing = combine_weights(fwd_numer[0])
    back_mixing = combine_weights(bwd_numer[0])
    unit_weights = jnp.ones_like(back_mixing)
    fwd_table = slot_table(fwd_positions, choices_per)
    back_table = slot_table(back_positions, choices_per)
    send_inputs = packed_rows(inputs, fwd_table)
    send_saved = packed_rows(saved, back_table)
    send_grad = packed_rows(grad_in, back_table, back_mixing)
    received, swapped_in = dispatch(
        (send_inputs, send_saved, send_grad),
        (
            lax.dynamic_slice_in_dim(down_half[0], theirs, half, 1),
            lax.dynamic_slice_in_dim(gate_half[0], theirs, half, 0),
            lax.dynamic_slice_in_dim(up_half[0], theirs, half, 0),
        ),
    )
    recv_inputs, recv_saved, recv_grad = (x.reshape(groups, 1, MOST, model_width) for x in received)
    down_recv, gate_recv, up_recv = (x[None] for x in swapped_in)
    down_mine = jnp.concatenate([lax.dynamic_slice_in_dim(down_half, mine, half, 2), down_recv], 1)
    gate_mine = jnp.concatenate([lax.dynamic_slice_in_dim(gate_half, mine, half, 1), gate_recv], 2)
    up_mine = jnp.concatenate([lax.dynamic_slice_in_dim(up_half, mine, half, 1), up_recv], 2)

    gate_value, up_value = project(recv_inputs, gate_half, up_half)
    hidden = (jax.nn.silu(gate_value) * up_value).astype(jnp.bfloat16)
    hidden_all = jnp.concatenate([hidden, swapped(hidden)], -1)
    out_part = jnp.einsum(
        "semf,efd->semd", hidden_all, down_mine, preferred_element_type=jnp.float32
    ).astype(jnp.bfloat16)

    back_gate, back_up = project(recv_saved, gate_half, up_half)
    back_hidden, gate_grad, up_grad = local_backward(back_gate, back_up, recv_grad, down_half)
    gate_term, up_term, down_term = weight_terms(
        recv_saved, recv_grad, back_hidden, gate_grad, up_grad
    )
    gate_other, up_other = swapped((gate_grad, up_grad))
    gate_all = jnp.concatenate([gate_grad, gate_other], -1)
    up_all = jnp.concatenate([up_grad, up_other], -1)
    grad_part = (
        jnp.einsum("semf,edf->semd", gate_all, gate_mine, preferred_element_type=jnp.float32)
        + jnp.einsum("semf,edf->semd", up_all, up_mine, preferred_element_type=jnp.float32)
    ).astype(jnp.bfloat16)

    back_out = lax.all_to_all(out_part, "expert", split_axis=0, concat_axis=0, tiled=True)
    back_grad = lax.all_to_all(grad_part, "expert", split_axis=0, concat_axis=0, tiled=True)
    inputs_part = lax.dynamic_slice_in_dim(inputs, mine, half, 1)
    grad_in_part = lax.dynamic_slice_in_dim(grad_in, mine, half, 1)
    layer_out = mix_rows(inputs_part, back_out, fwd_positions, mixing, choices_per)
    input_grad = mix_rows(grad_in_part, back_grad, back_positions, unit_weights, choices_per)
    layer_out = lax.all_gather(layer_out, "dp", axis=1, tiled=True)
    input_grad = lax.all_gather(input_grad, "dp", axis=1, tiled=True)
    next_fwd = handoff(layer_out[None], 1)
    next_bwd = handoff(input_grad[None], -1)
    gate_sum = gate_term.astype(jnp.bfloat16)
    up_sum = up_term.astype(jnp.bfloat16)
    down_sum = down_term.astype(jnp.bfloat16)
    return (next_fwd, next_bwd, gate_sum[None], up_sum[None], down_sum[None])


def solution(mesh):
    in_specs = (
        P("section", "expert", None),
        P("section", "expert", None),
        P("section", "expert", None),
        P("section", "expert", None),
        P("section", "expert", None),
        P("section", "expert", None),
        P("section", "expert", None),
        P("section", "expert", None, "dp"),
        P("section", "expert", None, "dp"),
        P("section", "expert", "dp", None),
    )
    out_specs = (
        P("section", "expert", None),
        P("section", "expert", None),
        P("section", "expert", None, "dp"),
        P("section", "expert", None, "dp"),
        P("section", "expert", "dp", None),
    )
    return jax.shard_map(local, mesh=mesh, in_specs=in_specs, out_specs=out_specs, check_vma=False)
```

```python
import functools

import jax
import jax.numpy as jnp
from jax import lax
from jax.experimental import pallas as pl
from jax.experimental.pallas import tpu as pltpu
from jax.sharding import PartitionSpec as P

MESH = pl.DeviceIdType.MESH

EXPERTS = 32
MOST = 26


def passed_along(block, axis, distance):
    devices = range(lax.axis_size(axis))
    route = [((i - distance) % len(devices), i) for i in devices]
    return lax.ppermute(block, axis, route)


def swapped(block):
    return lax.ppermute(block, "dp", [(0, 1), (1, 0)])


def exchange_kernel(n, spread, swapped_count, *refs):
    sends = refs[0:spread]
    swaps_out = refs[spread:spread + swapped_count]
    recvs = refs[spread + swapped_count:2 * spread + swapped_count]
    swaps_in = refs[2 * spread + swapped_count:2 * (spread + swapped_count)]
    send_sems, recv_sems, w_send, w_recv, local_sems = refs[2 * (spread + swapped_count):]
    me = lax.axis_index("expert")
    other = 1 - lax.axis_index("dp")

    barrier = pltpu.get_barrier_semaphore()

    def greet(o, carry):
        pl.semaphore_signal(barrier, 1, device_id={"expert": lax.rem(me + o, n)}, device_id_type=MESH)
        return carry

    lax.fori_loop(1, n, greet, 0)
    if swapped_count:
        pl.semaphore_signal(barrier, 1, device_id={"dp": other}, device_id_type=MESH)
    pl.semaphore_wait(barrier, n if swapped_count else n - 1)

    def copy_of(a, o):
        target = lax.rem(me + o, n)
        return pltpu.make_async_remote_copy(
            src_ref=sends[a].at[target],
            dst_ref=recvs[a].at[me],
            send_sem=send_sems.at[a, o],
            recv_sem=recv_sems.at[a, o],
            device_id={"expert": target},
            device_id_type=MESH,
        )

    swaps = [
        pltpu.make_async_remote_copy(
            src_ref=swaps_out[i],
            dst_ref=swaps_in[i],
            send_sem=w_send.at[i],
            recv_sem=w_recv.at[i],
            device_id={"dp": other},
            device_id_type=MESH,
        )
        for i in range(swapped_count)
    ]
    for swap in swaps:
        swap.start()
    locals_ = [
        pltpu.make_async_copy(sends[a].at[me], recvs[a].at[me], local_sems.at[a]) for a in range(spread)
    ]
    for a in range(spread):
        locals_[a].start()

        def start(o, carry, a=a):
            copy_of(a, o).start()
            return carry

        lax.fori_loop(1, n, start, 0)
    for a in range(spread):

        def finish(o, carry, a=a):
            copy_of(a, o).wait()
            return carry

        lax.fori_loop(1, n, finish, 0)
        locals_[a].wait()
    for swap in swaps:
        swap.wait()


def exchange(sends, swaps_out, collective_id):
    n = sends[0].shape[0]
    anywhere = pl.BlockSpec(memory_space=pl.ANY)
    arrays = (*sends, *swaps_out)
    moved = sum(x.size * x.dtype.itemsize for x in arrays)
    outs = pl.pallas_call(
        functools.partial(exchange_kernel, n, len(sends), len(swaps_out)),
        out_shape=[jax.ShapeDtypeStruct(x.shape, x.dtype) for x in arrays],
        in_specs=[anywhere] * len(arrays),
        out_specs=[anywhere] * len(arrays),
        scratch_shapes=[
            pltpu.SemaphoreType.DMA((len(sends), n)),
            pltpu.SemaphoreType.DMA((len(sends), n)),
            pltpu.SemaphoreType.DMA((max(1, len(swaps_out)),)),
            pltpu.SemaphoreType.DMA((max(1, len(swaps_out)),)),
            pltpu.SemaphoreType.DMA((len(sends),)),
        ],
        compiler_params=pltpu.CompilerParams(collective_id=collective_id, has_side_effects=True),
        cost_estimate=pl.CostEstimate(flops=0, bytes_accessed=2 * moved, transcendentals=0),
    )(*arrays)
    return outs[: len(sends)], outs[len(sends):]


def slot_ranks(routes):
    flat_routes = routes.reshape(-1)
    onehot_table = (flat_routes[:, None] == jnp.arange(EXPERTS, dtype=jnp.int32)[None, :]).astype(
        jnp.int32
    )
    earlier = jnp.cumsum(onehot_table, 0) - onehot_table
    return (flat_routes, jnp.sum(earlier * onehot_table, 1))


def combine_weights(numerators):
    counted = numerators.astype(jnp.float32)
    return counted / jnp.sum(counted, -1, keepdims=True)


def slot_table(positions, choices_per):
    slots = jnp.arange(EXPERTS * MOST, dtype=jnp.int32)
    return slots[:, None, None] == positions.reshape(-1, choices_per)[None, :, :]


def packed_rows(rows, table, scale=None):
    chosen = jnp.any(table, -1).reshape(EXPERTS, MOST, -1)
    picked = jnp.einsum("ecm,md->ecd", chosen.astype(rows.dtype), rows, preferred_element_type=jnp.float32)
    if scale is not None:
        picked = picked * jnp.sum(jnp.where(table, scale[None], 0.0), (1, 2)).reshape(EXPERTS, MOST, 1)
    return picked.astype(rows.dtype)


def handoff(value, direction):
    return passed_along(value, "section", direction)


def project(rows, gate_weight, up_weight):
    gate_value = jnp.einsum("semd,edf->semf", rows, gate_weight, preferred_element_type=jnp.float32)
    up_value = jnp.einsum("semd,edf->semf", rows, up_weight, preferred_element_type=jnp.float32)
    return (gate_value, up_value)


def local_backward(gate_value, up_value, grad_rows, down_weight):
    silu_gate = jax.nn.silu(gate_value)
    sigmoid_gate = jax.nn.sigmoid(gate_value)
    hidden = (silu_gate * up_value).astype(jnp.bfloat16)
    hidden_grad = jnp.einsum(
        "semd,efd->semf", grad_rows, down_weight, preferred_element_type=jnp.float32
    )
    up_grad = (hidden_grad * silu_gate).astype(jnp.bfloat16)
    gate_grad = (
        hidden_grad * up_value * sigmoid_gate * (1.0 + gate_value * (1.0 - sigmoid_gate))
    ).astype(jnp.bfloat16)
    return (hidden, gate_grad, up_grad)


def weight_terms(saved_rows, grad_rows, back_hidden, gate_grad, up_grad):
    gate_term = jnp.einsum(
        "semd,semf->edf", saved_rows, gate_grad, preferred_element_type=jnp.float32
    )
    up_term = jnp.einsum("semd,semf->edf", saved_rows, up_grad, preferred_element_type=jnp.float32)
    down_term = jnp.einsum(
        "semf,semd->efd", back_hidden, grad_rows, preferred_element_type=jnp.float32
    )
    return (gate_term, up_term, down_term)


def mix_rows(base, returned, positions, weights, choices_per):
    width = returned.shape[-1]
    picked = (
        returned.reshape(-1, width)[positions].reshape(-1, choices_per, width).astype(jnp.float32)
    )
    return (base.astype(jnp.float32) + jnp.sum(weights[:, :, None] * picked, 1)).astype(
        jnp.bfloat16
    )


def local(
    fwd_in, fwd_routes, fwd_numer, bwd_saved, bwd_routes, bwd_numer, bwd_grad, w_gate, w_up, w_down
):
    groups = lax.axis_size("expert")
    inputs = fwd_in[0]
    saved = bwd_saved[0]
    grad_in = bwd_grad[0]
    model_width = inputs.shape[-1]
    half = model_width // lax.axis_size("dp")
    mine = lax.axis_index("dp") * half
    theirs = half - mine
    choices_per = fwd_routes.shape[-1]
    gate_half = w_gate[0]
    up_half = w_up[0]
    down_half = w_down[0]

    fwd_flat, fwd_rank = slot_ranks(fwd_routes[0])
    back_flat, back_rank = slot_ranks(bwd_routes[0])
    fwd_positions = fwd_flat * MOST + fwd_rank
    back_positions = back_flat * MOST + back_rank
    mixing = combine_weights(fwd_numer[0])
    back_mixing = combine_weights(bwd_numer[0])
    unit_weights = jnp.ones_like(back_mixing)
    fwd_table = slot_table(fwd_positions, choices_per)
    back_table = slot_table(back_positions, choices_per)
    send_inputs = packed_rows(inputs, fwd_table)
    send_saved = packed_rows(saved, back_table)
    send_grad = packed_rows(grad_in, back_table, back_mixing)
    (recv_saved, recv_grad), swapped_in = exchange(
        (send_saved, send_grad),
        (
            lax.dynamic_slice_in_dim(down_half[0], theirs, half, 1),
            lax.dynamic_slice_in_dim(gate_half[0], theirs, half, 0),
            lax.dynamic_slice_in_dim(up_half[0], theirs, half, 0),
        ),
        0,
    )
    recv_saved, recv_grad = (x.reshape(groups, 1, MOST, model_width) for x in (recv_saved, recv_grad))
    down_recv, gate_recv, up_recv = (x[None] for x in swapped_in)
    down_mine = jnp.concatenate([lax.dynamic_slice_in_dim(down_half, mine, half, 2), down_recv], 1)
    gate_mine = jnp.concatenate([lax.dynamic_slice_in_dim(gate_half, mine, half, 1), gate_recv], 2)
    up_mine = jnp.concatenate([lax.dynamic_slice_in_dim(up_half, mine, half, 1), up_recv], 2)

    back_gate, back_up = project(recv_saved, gate_half, up_half)
    back_hidden, gate_grad, up_grad = local_backward(back_gate, back_up, recv_grad, down_half)
    gate_term, up_term, down_term = weight_terms(
        recv_saved, recv_grad, back_hidden, gate_grad, up_grad
    )
    (recv_inputs,), (gate_other, up_other) = exchange((send_inputs,), (gate_grad, up_grad), 1)
    recv_inputs = recv_inputs.reshape(groups, 1, MOST, model_width)
    gate_all = jnp.concatenate([gate_grad, gate_other], -1)
    up_all = jnp.concatenate([up_grad, up_other], -1)
    grad_part = (
        jnp.einsum("semf,edf->semd", gate_all, gate_mine, preferred_element_type=jnp.float32)
        + jnp.einsum("semf,edf->semd", up_all, up_mine, preferred_element_type=jnp.float32)
    ).astype(jnp.bfloat16)

    gate_value, up_value = project(recv_inputs, gate_half, up_half)
    hidden = (jax.nn.silu(gate_value) * up_value).astype(jnp.bfloat16)
    (back_grad,), (hidden_other,) = exchange((grad_part.reshape(groups, MOST, half),), (hidden,), 2)
    hidden_all = jnp.concatenate([hidden, hidden_other], -1)
    out_part = jnp.einsum(
        "semf,efd->semd", hidden_all, down_mine, preferred_element_type=jnp.float32
    ).astype(jnp.bfloat16)
    (back_out,), _ = exchange((out_part.reshape(groups, MOST, half),), (), 3)
    inputs_part = lax.dynamic_slice_in_dim(inputs, mine, half, 1)
    grad_in_part = lax.dynamic_slice_in_dim(grad_in, mine, half, 1)
    layer_out = mix_rows(inputs_part, back_out, fwd_positions, mixing, choices_per)
    input_grad = mix_rows(grad_in_part, back_grad, back_positions, unit_weights, choices_per)
    layer_out = lax.all_gather(layer_out, "dp", axis=1, tiled=True)
    input_grad = lax.all_gather(input_grad, "dp", axis=1, tiled=True)
    next_fwd = handoff(layer_out[None], 1)
    next_bwd = handoff(input_grad[None], -1)
    gate_sum = gate_term.astype(jnp.bfloat16)
    up_sum = up_term.astype(jnp.bfloat16)
    down_sum = down_term.astype(jnp.bfloat16)
    return (next_fwd, next_bwd, gate_sum[None], up_sum[None], down_sum[None])


def solution(mesh):
    in_specs = (
        P("section", "expert", None),
        P("section", "expert", None),
        P("section", "expert", None),
        P("section", "expert", None),
        P("section", "expert", None),
        P("section", "expert", None),
        P("section", "expert", None),
        P("section", "expert", None, "dp"),
        P("section", "expert", None, "dp"),
        P("section", "expert", "dp", None),
    )
    out_specs = (
        P("section", "expert", None),
        P("section", "expert", None),
        P("section", "expert", None, "dp"),
        P("section", "expert", None, "dp"),
        P("section", "expert", "dp", None),
    )
    return jax.shard_map(local, mesh=mesh, in_specs=in_specs, out_specs=out_specs, check_vma=False)
```

```python
import functools

import jax
import jax.numpy as jnp
from jax import lax
from jax.experimental import pallas as pl
from jax.experimental.pallas import tpu as pltpu
from jax.sharding import PartitionSpec as P

MESH = pl.DeviceIdType.MESH

EXPERTS = 32
MOST = 26


def passed_along(block, axis, distance):
    devices = range(lax.axis_size(axis))
    route = [((i - distance) % len(devices), i) for i in devices]
    return lax.ppermute(block, axis, route)


def swapped(block):
    return lax.ppermute(block, "dp", [(0, 1), (1, 0)])


def exchange_kernel(n, spread, swapped_count, *refs):
    sends = refs[0:spread]
    swaps_out = refs[spread:spread + swapped_count]
    recvs = refs[spread + swapped_count:2 * spread + swapped_count]
    swaps_in = refs[2 * spread + swapped_count:2 * (spread + swapped_count)]
    send_sems, recv_sems, w_send, w_recv, local_sems = refs[2 * (spread + swapped_count):]
    me = lax.axis_index("expert")
    other = 1 - lax.axis_index("dp")

    barrier = pltpu.get_barrier_semaphore()

    def greet(o, carry):
        pl.semaphore_signal(barrier, 1, device_id={"expert": lax.rem(me + o, n)}, device_id_type=MESH)
        return carry

    lax.fori_loop(1, n, greet, 0)
    if swapped_count:
        pl.semaphore_signal(barrier, 1, device_id={"dp": other}, device_id_type=MESH)
    pl.semaphore_wait(barrier, n if swapped_count else n - 1)

    def copy_of(a, o):
        target = lax.rem(me + o, n)
        return pltpu.make_async_remote_copy(
            src_ref=sends[a].at[target],
            dst_ref=recvs[a].at[me],
            send_sem=send_sems.at[a, o],
            recv_sem=recv_sems.at[a, o],
            device_id={"expert": target},
            device_id_type=MESH,
        )

    swaps = [
        pltpu.make_async_remote_copy(
            src_ref=swaps_out[i],
            dst_ref=swaps_in[i],
            send_sem=w_send.at[i],
            recv_sem=w_recv.at[i],
            device_id={"dp": other},
            device_id_type=MESH,
        )
        for i in range(swapped_count)
    ]
    for swap in swaps:
        swap.start()
    locals_ = [
        pltpu.make_async_copy(sends[a].at[me], recvs[a].at[me], local_sems.at[a]) for a in range(spread)
    ]
    for a in range(spread):
        locals_[a].start()

        def start(o, carry, a=a):
            copy_of(a, o).start()
            return carry

        lax.fori_loop(1, n, start, 0)
    for a in range(spread):

        def finish(o, carry, a=a):
            copy_of(a, o).wait()
            return carry

        lax.fori_loop(1, n, finish, 0)
        locals_[a].wait()
    for swap in swaps:
        swap.wait()


def exchange(sends, swaps_out, collective_id):
    n = sends[0].shape[0]
    anywhere = pl.BlockSpec(memory_space=pl.ANY)
    arrays = (*sends, *swaps_out)
    moved = sum(x.size * x.dtype.itemsize for x in arrays)
    outs = pl.pallas_call(
        functools.partial(exchange_kernel, n, len(sends), len(swaps_out)),
        out_shape=[jax.ShapeDtypeStruct(x.shape, x.dtype) for x in arrays],
        in_specs=[anywhere] * len(arrays),
        out_specs=[anywhere] * len(arrays),
        scratch_shapes=[
            pltpu.SemaphoreType.DMA((len(sends), n)),
            pltpu.SemaphoreType.DMA((len(sends), n)),
            pltpu.SemaphoreType.DMA((max(1, len(swaps_out)),)),
            pltpu.SemaphoreType.DMA((max(1, len(swaps_out)),)),
            pltpu.SemaphoreType.DMA((len(sends),)),
        ],
        compiler_params=pltpu.CompilerParams(collective_id=collective_id, has_side_effects=True),
        cost_estimate=pl.CostEstimate(flops=0, bytes_accessed=2 * moved, transcendentals=0),
    )(*arrays)
    return outs[: len(sends)], outs[len(sends):]


def slot_ranks(routes):
    flat_routes = routes.reshape(-1)
    onehot_table = (flat_routes[:, None] == jnp.arange(EXPERTS, dtype=jnp.int32)[None, :]).astype(
        jnp.int32
    )
    earlier = jnp.cumsum(onehot_table, 0) - onehot_table
    return (flat_routes, jnp.sum(earlier * onehot_table, 1))


def combine_weights(numerators):
    counted = numerators.astype(jnp.float32)
    return counted / jnp.sum(counted, -1, keepdims=True)


def slot_table(positions, choices_per):
    slots = jnp.arange(EXPERTS * MOST, dtype=jnp.int32)
    return slots[:, None, None] == positions.reshape(-1, choices_per)[None, :, :]


def packed_rows(rows, table, scale=None):
    chosen = jnp.any(table, -1).reshape(EXPERTS, MOST, -1)
    picked = jnp.einsum("ecm,md->ecd", chosen.astype(rows.dtype), rows, preferred_element_type=jnp.float32)
    if scale is not None:
        picked = picked * jnp.sum(jnp.where(table, scale[None], 0.0), (1, 2)).reshape(EXPERTS, MOST, 1)
    return picked.astype(rows.dtype)


def handoff(value, direction):
    return passed_along(value, "section", direction)


def project(rows, gate_weight, up_weight):
    gate_value = jnp.einsum("semd,edf->semf", rows, gate_weight, preferred_element_type=jnp.float32)
    up_value = jnp.einsum("semd,edf->semf", rows, up_weight, preferred_element_type=jnp.float32)
    return (gate_value, up_value)


def local_backward(gate_value, up_value, grad_rows, down_weight):
    silu_gate = jax.nn.silu(gate_value)
    sigmoid_gate = jax.nn.sigmoid(gate_value)
    hidden = (silu_gate * up_value).astype(jnp.bfloat16)
    hidden_grad = jnp.einsum(
        "semd,efd->semf", grad_rows, down_weight, preferred_element_type=jnp.float32
    )
    up_grad = (hidden_grad * silu_gate).astype(jnp.bfloat16)
    gate_grad = (
        hidden_grad * up_value * sigmoid_gate * (1.0 + gate_value * (1.0 - sigmoid_gate))
    ).astype(jnp.bfloat16)
    return (hidden, gate_grad, up_grad)


def weight_terms(saved_rows, grad_rows, back_hidden, gate_grad, up_grad):
    gate_term = jnp.einsum(
        "semd,semf->edf", saved_rows, gate_grad, preferred_element_type=jnp.float32
    )
    up_term = jnp.einsum("semd,semf->edf", saved_rows, up_grad, preferred_element_type=jnp.float32)
    down_term = jnp.einsum(
        "semf,semd->efd", back_hidden, grad_rows, preferred_element_type=jnp.float32
    )
    return (gate_term, up_term, down_term)


def mix_rows(base, returned, positions, weights, choices_per):
    width = returned.shape[-1]
    picked = (
        returned.reshape(-1, width)[positions].reshape(-1, choices_per, width).astype(jnp.float32)
    )
    return (base.astype(jnp.float32) + jnp.sum(weights[:, :, None] * picked, 1)).astype(
        jnp.bfloat16
    )


def local(
    fwd_in, fwd_routes, fwd_numer, bwd_saved, bwd_routes, bwd_numer, bwd_grad, w_gate, w_up, w_down
):
    groups = lax.axis_size("expert")
    inputs = fwd_in[0]
    saved = bwd_saved[0]
    grad_in = bwd_grad[0]
    model_width = inputs.shape[-1]
    half = model_width // lax.axis_size("dp")
    mine = lax.axis_index("dp") * half
    theirs = half - mine
    choices_per = fwd_routes.shape[-1]
    gate_half = w_gate[0]
    up_half = w_up[0]
    down_half = w_down[0]

    fwd_flat, fwd_rank = slot_ranks(fwd_routes[0])
    back_flat, back_rank = slot_ranks(bwd_routes[0])
    fwd_positions = fwd_flat * MOST + fwd_rank
    back_positions = back_flat * MOST + back_rank
    mixing = combine_weights(fwd_numer[0])
    back_mixing = combine_weights(bwd_numer[0])
    unit_weights = jnp.ones_like(back_mixing)
    fwd_table = slot_table(fwd_positions, choices_per)
    back_table = slot_table(back_positions, choices_per)
    send_inputs = packed_rows(inputs, fwd_table)
    (recv_inputs,), swapped_in = exchange(
        (send_inputs,),
        (
            lax.dynamic_slice_in_dim(down_half[0], theirs, half, 1),
            lax.dynamic_slice_in_dim(gate_half[0], theirs, half, 0),
            lax.dynamic_slice_in_dim(up_half[0], theirs, half, 0),
        ),
        0,
    )
    recv_inputs = recv_inputs.reshape(groups, 1, MOST, model_width)
    down_recv, gate_recv, up_recv = (x[None] for x in swapped_in)
    down_mine = jnp.concatenate([lax.dynamic_slice_in_dim(down_half, mine, half, 2), down_recv], 1)
    gate_mine = jnp.concatenate([lax.dynamic_slice_in_dim(gate_half, mine, half, 1), gate_recv], 2)
    up_mine = jnp.concatenate([lax.dynamic_slice_in_dim(up_half, mine, half, 1), up_recv], 2)
    send_saved = packed_rows(saved, back_table).reshape(groups, 1, MOST, model_width)
    send_grad = packed_rows(grad_in, back_table, back_mixing).reshape(groups, 1, MOST, model_width)
    recv_saved = lax.all_to_all(send_saved, "expert", split_axis=0, concat_axis=0, tiled=True)
    recv_grad = lax.all_to_all(send_grad, "expert", split_axis=0, concat_axis=0, tiled=True)

    gate_value, up_value = project(recv_inputs, gate_half, up_half)
    hidden = (jax.nn.silu(gate_value) * up_value).astype(jnp.bfloat16)
    hidden_all = jnp.concatenate([hidden, swapped(hidden)], -1)
    out_part = jnp.einsum(
        "semf,efd->semd", hidden_all, down_mine, preferred_element_type=jnp.float32
    ).astype(jnp.bfloat16)

    back_gate, back_up = project(recv_saved, gate_half, up_half)
    back_hidden, gate_grad, up_grad = local_backward(back_gate, back_up, recv_grad, down_half)
    gate_term, up_term, down_term = weight_terms(
        recv_saved, recv_grad, back_hidden, gate_grad, up_grad
    )
    gate_other, up_other = swapped((gate_grad, up_grad))
    gate_all = jnp.concatenate([gate_grad, gate_other], -1)
    up_all = jnp.concatenate([up_grad, up_other], -1)
    grad_part = (
        jnp.einsum("semf,edf->semd", gate_all, gate_mine, preferred_element_type=jnp.float32)
        + jnp.einsum("semf,edf->semd", up_all, up_mine, preferred_element_type=jnp.float32)
    ).astype(jnp.bfloat16)

    back_out = lax.all_to_all(out_part, "expert", split_axis=0, concat_axis=0, tiled=True)
    back_grad = lax.all_to_all(grad_part, "expert", split_axis=0, concat_axis=0, tiled=True)
    inputs_part = lax.dynamic_slice_in_dim(inputs, mine, half, 1)
    grad_in_part = lax.dynamic_slice_in_dim(grad_in, mine, half, 1)
    layer_out = mix_rows(inputs_part, back_out, fwd_positions, mixing, choices_per)
    input_grad = mix_rows(grad_in_part, back_grad, back_positions, unit_weights, choices_per)
    layer_out = lax.all_gather(layer_out, "dp", axis=1, tiled=True)
    input_grad = lax.all_gather(input_grad, "dp", axis=1, tiled=True)
    next_fwd = handoff(layer_out[None], 1)
    next_bwd = handoff(input_grad[None], -1)
    gate_sum = gate_term.astype(jnp.bfloat16)
    up_sum = up_term.astype(jnp.bfloat16)
    down_sum = down_term.astype(jnp.bfloat16)
    return (next_fwd, next_bwd, gate_sum[None], up_sum[None], down_sum[None])


def solution(mesh):
    in_specs = (
        P("section", "expert", None),
        P("section", "expert", None),
        P("section", "expert", None),
        P("section", "expert", None),
        P("section", "expert", None),
        P("section", "expert", None),
        P("section", "expert", None),
        P("section", "expert", None, "dp"),
        P("section", "expert", None, "dp"),
        P("section", "expert", "dp", None),
    )
    out_specs = (
        P("section", "expert", None),
        P("section", "expert", None),
        P("section", "expert", None, "dp"),
        P("section", "expert", None, "dp"),
        P("section", "expert", "dp", None),
    )
    return jax.shard_map(local, mesh=mesh, in_specs=in_specs, out_specs=out_specs, check_vma=False)
```

```python
import functools

import jax
import jax.numpy as jnp
from jax import lax
from jax.experimental import pallas as pl
from jax.experimental.pallas import tpu as pltpu
from jax.sharding import PartitionSpec as P

MESH = pl.DeviceIdType.MESH

EXPERTS = 32
MOST = 26


def passed_along(block, axis, distance):
    devices = range(lax.axis_size(axis))
    route = [((i - distance) % len(devices), i) for i in devices]
    return lax.ppermute(block, axis, route)


def swapped(block):
    return lax.ppermute(block, "dp", [(0, 1), (1, 0)])


def exchange_kernel(n, spread, swapped_count, *refs):
    sends = refs[0:spread]
    swaps_out = refs[spread:spread + swapped_count]
    recvs = refs[spread + swapped_count:2 * spread + swapped_count]
    swaps_in = refs[2 * spread + swapped_count:2 * (spread + swapped_count)]
    send_sems, recv_sems, w_send, w_recv, local_sems = refs[2 * (spread + swapped_count):]
    me = lax.axis_index("expert")
    other = 1 - lax.axis_index("dp")

    barrier = pltpu.get_barrier_semaphore()

    def greet(o, carry):
        pl.semaphore_signal(barrier, 1, device_id={"expert": lax.rem(me + o, n)}, device_id_type=MESH)
        return carry

    lax.fori_loop(1, n, greet, 0)
    if swapped_count:
        pl.semaphore_signal(barrier, 1, device_id={"dp": other}, device_id_type=MESH)
    pl.semaphore_wait(barrier, n if swapped_count else n - 1)

    def copy_of(a, o):
        target = lax.rem(me + o, n)
        return pltpu.make_async_remote_copy(
            src_ref=sends[a].at[target],
            dst_ref=recvs[a].at[me],
            send_sem=send_sems.at[a, o],
            recv_sem=recv_sems.at[a, o],
            device_id={"expert": target},
            device_id_type=MESH,
        )

    swaps = [
        pltpu.make_async_remote_copy(
            src_ref=swaps_out[i],
            dst_ref=swaps_in[i],
            send_sem=w_send.at[i],
            recv_sem=w_recv.at[i],
            device_id={"dp": other},
            device_id_type=MESH,
        )
        for i in range(swapped_count)
    ]
    for swap in swaps:
        swap.start()
    locals_ = [
        pltpu.make_async_copy(sends[a].at[me], recvs[a].at[me], local_sems.at[a]) for a in range(spread)
    ]
    for a in range(spread):
        locals_[a].start()

        def start(o, carry, a=a):
            copy_of(a, o).start()
            return carry

        lax.fori_loop(1, n, start, 0)
    for a in range(spread):

        def finish(o, carry, a=a):
            copy_of(a, o).wait()
            return carry

        lax.fori_loop(1, n, finish, 0)
        locals_[a].wait()
    for swap in swaps:
        swap.wait()


def exchange(sends, swaps_out, collective_id):
    n = sends[0].shape[0]
    anywhere = pl.BlockSpec(memory_space=pl.ANY)
    arrays = (*sends, *swaps_out)
    moved = sum(x.size * x.dtype.itemsize for x in arrays)
    outs = pl.pallas_call(
        functools.partial(exchange_kernel, n, len(sends), len(swaps_out)),
        out_shape=[jax.ShapeDtypeStruct(x.shape, x.dtype) for x in arrays],
        in_specs=[anywhere] * len(arrays),
        out_specs=[anywhere] * len(arrays),
        scratch_shapes=[
            pltpu.SemaphoreType.DMA((len(sends), n)),
            pltpu.SemaphoreType.DMA((len(sends), n)),
            pltpu.SemaphoreType.DMA((max(1, len(swaps_out)),)),
            pltpu.SemaphoreType.DMA((max(1, len(swaps_out)),)),
            pltpu.SemaphoreType.DMA((len(sends),)),
        ],
        compiler_params=pltpu.CompilerParams(collective_id=collective_id, has_side_effects=True),
        cost_estimate=pl.CostEstimate(flops=0, bytes_accessed=2 * moved, transcendentals=0),
    )(*arrays)
    return outs[: len(sends)], outs[len(sends):]


def slot_ranks(routes):
    flat_routes = routes.reshape(-1)
    onehot_table = (flat_routes[:, None] == jnp.arange(EXPERTS, dtype=jnp.int32)[None, :]).astype(
        jnp.int32
    )
    earlier = jnp.cumsum(onehot_table, 0) - onehot_table
    return (flat_routes, jnp.sum(earlier * onehot_table, 1))


def combine_weights(numerators):
    counted = numerators.astype(jnp.float32)
    return counted / jnp.sum(counted, -1, keepdims=True)


def slot_table(positions, choices_per):
    slots = jnp.arange(EXPERTS * MOST, dtype=jnp.int32)
    return slots[:, None, None] == positions.reshape(-1, choices_per)[None, :, :]


def packed_rows(rows, table, scale=None):
    chosen = jnp.any(table, -1).reshape(EXPERTS, MOST, -1)
    picked = jnp.einsum("ecm,md->ecd", chosen.astype(rows.dtype), rows, preferred_element_type=jnp.float32)
    if scale is not None:
        picked = picked * jnp.sum(jnp.where(table, scale[None], 0.0), (1, 2)).reshape(EXPERTS, MOST, 1)
    return picked.astype(rows.dtype)


def handoff(value, direction):
    sections = lax.axis_size("section")
    same = passed_along(value, "section", direction)
    route = [(i * 2 + j, ((i + direction) % sections) * 2 + 1 - j) for i in range(sections) for j in range(2)]
    crossed = lax.ppermute(value, ("section", "dp"), route)
    first = lax.axis_index("dp") == 0
    return jnp.concatenate([jnp.where(first, same, crossed), jnp.where(first, crossed, same)], 1)


def project(rows, gate_weight, up_weight):
    gate_value = jnp.einsum("semd,edf->semf", rows, gate_weight, preferred_element_type=jnp.float32)
    up_value = jnp.einsum("semd,edf->semf", rows, up_weight, preferred_element_type=jnp.float32)
    return (gate_value, up_value)


def local_backward(gate_value, up_value, grad_rows, down_weight):
    silu_gate = jax.nn.silu(gate_value)
    sigmoid_gate = jax.nn.sigmoid(gate_value)
    hidden = (silu_gate * up_value).astype(jnp.bfloat16)
    hidden_grad = jnp.einsum(
        "semd,efd->semf", grad_rows, down_weight, preferred_element_type=jnp.float32
    )
    up_grad = (hidden_grad * silu_gate).astype(jnp.bfloat16)
    gate_grad = (
        hidden_grad * up_value * sigmoid_gate * (1.0 + gate_value * (1.0 - sigmoid_gate))
    ).astype(jnp.bfloat16)
    return (hidden, gate_grad, up_grad)


def weight_terms(saved_rows, grad_rows, back_hidden, gate_grad, up_grad):
    gate_term = jnp.einsum(
        "semd,semf->edf", saved_rows, gate_grad, preferred_element_type=jnp.float32
    )
    up_term = jnp.einsum("semd,semf->edf", saved_rows, up_grad, preferred_element_type=jnp.float32)
    down_term = jnp.einsum(
        "semf,semd->efd", back_hidden, grad_rows, preferred_element_type=jnp.float32
    )
    return (gate_term, up_term, down_term)


def mix_rows(base, returned, positions, weights, choices_per):
    width = returned.shape[-1]
    picked = (
        returned.reshape(-1, width)[positions].reshape(-1, choices_per, width).astype(jnp.float32)
    )
    return (base.astype(jnp.float32) + jnp.sum(weights[:, :, None] * picked, 1)).astype(
        jnp.bfloat16
    )


def local(
    fwd_in, fwd_routes, fwd_numer, bwd_saved, bwd_routes, bwd_numer, bwd_grad, w_gate, w_up, w_down
):
    groups = lax.axis_size("expert")
    inputs = fwd_in[0]
    saved = bwd_saved[0]
    grad_in = bwd_grad[0]
    model_width = inputs.shape[-1]
    half = model_width // lax.axis_size("dp")
    mine = lax.axis_index("dp") * half
    theirs = half - mine
    choices_per = fwd_routes.shape[-1]
    gate_half = w_gate[0]
    up_half = w_up[0]
    down_half = w_down[0]

    fwd_flat, fwd_rank = slot_ranks(fwd_routes[0])
    back_flat, back_rank = slot_ranks(bwd_routes[0])
    fwd_positions = fwd_flat * MOST + fwd_rank
    back_positions = back_flat * MOST + back_rank
    mixing = combine_weights(fwd_numer[0])
    back_mixing = combine_weights(bwd_numer[0])
    unit_weights = jnp.ones_like(back_mixing)
    fwd_table = slot_table(fwd_positions, choices_per)
    back_table = slot_table(back_positions, choices_per)
    send_inputs = packed_rows(inputs, fwd_table)
    (recv_inputs,), swapped_in = exchange(
        (send_inputs,),
        (
            lax.dynamic_slice_in_dim(down_half[0], theirs, half, 1),
            lax.dynamic_slice_in_dim(gate_half[0], theirs, half, 0),
            lax.dynamic_slice_in_dim(up_half[0], theirs, half, 0),
        ),
        0,
    )
    recv_inputs = recv_inputs.reshape(groups, 1, MOST, model_width)
    down_recv, gate_recv, up_recv = (x[None] for x in swapped_in)
    down_mine = jnp.concatenate([lax.dynamic_slice_in_dim(down_half, mine, half, 2), down_recv], 1)
    gate_mine = jnp.concatenate([lax.dynamic_slice_in_dim(gate_half, mine, half, 1), gate_recv], 2)
    up_mine = jnp.concatenate([lax.dynamic_slice_in_dim(up_half, mine, half, 1), up_recv], 2)
    send_saved = packed_rows(saved, back_table).reshape(groups, 1, MOST, model_width)
    send_grad = packed_rows(grad_in, back_table, back_mixing).reshape(groups, 1, MOST, model_width)
    recv_inputs, send_saved, send_grad = lax.optimization_barrier((recv_inputs, send_saved, send_grad))
    recv_saved = lax.all_to_all(send_saved, "expert", split_axis=0, concat_axis=0, tiled=True)
    recv_grad = lax.all_to_all(send_grad, "expert", split_axis=0, concat_axis=0, tiled=True)

    gate_value, up_value = project(recv_inputs, gate_half, up_half)
    hidden = (jax.nn.silu(gate_value) * up_value).astype(jnp.bfloat16)
    hidden_all = jnp.concatenate([hidden, swapped(hidden)], -1)
    out_part = jnp.einsum(
        "semf,efd->semd", hidden_all, down_mine, preferred_element_type=jnp.float32
    ).astype(jnp.bfloat16)

    back_gate, back_up = project(recv_saved, gate_half, up_half)
    back_hidden, gate_grad, up_grad = local_backward(back_gate, back_up, recv_grad, down_half)
    gate_term, up_term, down_term = weight_terms(
        recv_saved, recv_grad, back_hidden, gate_grad, up_grad
    )
    gate_other, up_other = swapped((gate_grad, up_grad))
    gate_all = jnp.concatenate([gate_grad, gate_other], -1)
    up_all = jnp.concatenate([up_grad, up_other], -1)
    grad_part = (
        jnp.einsum("semf,edf->semd", gate_all, gate_mine, preferred_element_type=jnp.float32)
        + jnp.einsum("semf,edf->semd", up_all, up_mine, preferred_element_type=jnp.float32)
    ).astype(jnp.bfloat16)

    back_out = lax.all_to_all(out_part, "expert", split_axis=0, concat_axis=0, tiled=True)
    back_grad = lax.all_to_all(grad_part, "expert", split_axis=0, concat_axis=0, tiled=True)
    inputs_part = lax.dynamic_slice_in_dim(inputs, mine, half, 1)
    grad_in_part = lax.dynamic_slice_in_dim(grad_in, mine, half, 1)
    layer_out = mix_rows(inputs_part, back_out, fwd_positions, mixing, choices_per)
    input_grad = mix_rows(grad_in_part, back_grad, back_positions, unit_weights, choices_per)
    next_fwd = handoff(layer_out, 1)[None]
    next_bwd = handoff(input_grad, -1)[None]
    gate_sum = gate_term.astype(jnp.bfloat16)
    up_sum = up_term.astype(jnp.bfloat16)
    down_sum = down_term.astype(jnp.bfloat16)
    return (next_fwd, next_bwd, gate_sum[None], up_sum[None], down_sum[None])


def solution(mesh):
    in_specs = (
        P("section", "expert", None),
        P("section", "expert", None),
        P("section", "expert", None),
        P("section", "expert", None),
        P("section", "expert", None),
        P("section", "expert", None),
        P("section", "expert", None),
        P("section", "expert", None, "dp"),
        P("section", "expert", None, "dp"),
        P("section", "expert", "dp", None),
    )
    out_specs = (
        P("section", "expert", None),
        P("section", "expert", None),
        P("section", "expert", None, "dp"),
        P("section", "expert", None, "dp"),
        P("section", "expert", "dp", None),
    )
    return jax.shard_map(local, mesh=mesh, in_specs=in_specs, out_specs=out_specs, check_vma=False)
```

```python
import functools

import jax
import jax.numpy as jnp
from jax import lax
from jax.experimental import pallas as pl
from jax.experimental.pallas import tpu as pltpu
from jax.sharding import PartitionSpec as P

MESH = pl.DeviceIdType.MESH

EXPERTS = 32
MOST = 26


def passed_along(block, axis, distance):
    devices = range(lax.axis_size(axis))
    route = [((i - distance) % len(devices), i) for i in devices]
    return lax.ppermute(block, axis, route)


def swapped(block):
    return lax.ppermute(block, "dp", [(0, 1), (1, 0)])


def exchange_kernel(n, spread, swapped_count, *refs):
    sends = refs[0:spread]
    swaps_out = refs[spread:spread + swapped_count]
    recvs = refs[spread + swapped_count:2 * spread + swapped_count]
    swaps_in = refs[2 * spread + swapped_count:2 * (spread + swapped_count)]
    send_sems, recv_sems, w_send, w_recv, local_sems = refs[2 * (spread + swapped_count):]
    me = lax.axis_index("expert")
    other = 1 - lax.axis_index("dp")

    barrier = pltpu.get_barrier_semaphore()

    def greet(o, carry):
        pl.semaphore_signal(barrier, 1, device_id={"expert": lax.rem(me + o, n)}, device_id_type=MESH)
        return carry

    lax.fori_loop(1, n, greet, 0)
    if swapped_count:
        pl.semaphore_signal(barrier, 1, device_id={"dp": other}, device_id_type=MESH)
    pl.semaphore_wait(barrier, n if swapped_count else n - 1)

    def copy_of(a, o):
        target = lax.rem(me + o, n)
        return pltpu.make_async_remote_copy(
            src_ref=sends[a].at[target],
            dst_ref=recvs[a].at[me],
            send_sem=send_sems.at[a, o],
            recv_sem=recv_sems.at[a, o],
            device_id={"expert": target},
            device_id_type=MESH,
        )

    swaps = [
        pltpu.make_async_remote_copy(
            src_ref=swaps_out[i],
            dst_ref=swaps_in[i],
            send_sem=w_send.at[i],
            recv_sem=w_recv.at[i],
            device_id={"dp": other},
            device_id_type=MESH,
        )
        for i in range(swapped_count)
    ]
    for swap in swaps:
        swap.start()
    locals_ = [
        pltpu.make_async_copy(sends[a].at[me], recvs[a].at[me], local_sems.at[a]) for a in range(spread)
    ]
    for a in range(spread):
        locals_[a].start()

        def start(o, carry, a=a):
            copy_of(a, o).start()
            return carry

        lax.fori_loop(1, n, start, 0)
    for a in range(spread):

        def finish(o, carry, a=a):
            copy_of(a, o).wait()
            return carry

        lax.fori_loop(1, n, finish, 0)
        locals_[a].wait()
    for swap in swaps:
        swap.wait()


def exchange(sends, swaps_out, collective_id):
    n = sends[0].shape[0]
    anywhere = pl.BlockSpec(memory_space=pl.ANY)
    arrays = (*sends, *swaps_out)
    moved = sum(x.size * x.dtype.itemsize for x in arrays)
    outs = pl.pallas_call(
        functools.partial(exchange_kernel, n, len(sends), len(swaps_out)),
        out_shape=[jax.ShapeDtypeStruct(x.shape, x.dtype) for x in arrays],
        in_specs=[anywhere] * len(arrays),
        out_specs=[anywhere] * len(arrays),
        scratch_shapes=[
            pltpu.SemaphoreType.DMA((len(sends), n)),
            pltpu.SemaphoreType.DMA((len(sends), n)),
            pltpu.SemaphoreType.DMA((max(1, len(swaps_out)),)),
            pltpu.SemaphoreType.DMA((max(1, len(swaps_out)),)),
            pltpu.SemaphoreType.DMA((len(sends),)),
        ],
        compiler_params=pltpu.CompilerParams(collective_id=collective_id, has_side_effects=True),
        cost_estimate=pl.CostEstimate(flops=0, bytes_accessed=2 * moved, transcendentals=0),
    )(*arrays)
    return outs[: len(sends)], outs[len(sends):]


def slot_ranks(routes):
    flat_routes = routes.reshape(-1)
    onehot_table = (flat_routes[:, None] == jnp.arange(EXPERTS, dtype=jnp.int32)[None, :]).astype(
        jnp.int32
    )
    earlier = jnp.cumsum(onehot_table, 0) - onehot_table
    return (flat_routes, jnp.sum(earlier * onehot_table, 1))


def combine_weights(numerators):
    counted = numerators.astype(jnp.float32)
    return counted / jnp.sum(counted, -1, keepdims=True)


def slot_table(positions, choices_per, depth=MOST):
    slots = jnp.arange(EXPERTS * depth, dtype=jnp.int32)
    return slots[:, None, None] == positions.reshape(-1, choices_per)[None, :, :]


def packed_rows(rows, table, scale=None, depth=MOST):
    chosen = jnp.any(table, -1).reshape(EXPERTS, depth, -1)
    picked = jnp.einsum("ecm,md->ecd", chosen.astype(rows.dtype), rows, preferred_element_type=jnp.float32)
    if scale is not None:
        picked = picked * jnp.sum(jnp.where(table, scale[None], 0.0), (1, 2)).reshape(EXPERTS, depth, 1)
    return picked.astype(rows.dtype)


def handoff(value, direction):
    sections = lax.axis_size("section")
    same = passed_along(value, "section", direction)
    route = [(i * 2 + j, ((i + direction) % sections) * 2 + 1 - j) for i in range(sections) for j in range(2)]
    crossed = lax.ppermute(value, ("section", "dp"), route)
    first = lax.axis_index("dp") == 0
    return jnp.concatenate([jnp.where(first, same, crossed), jnp.where(first, crossed, same)], 1)


def project(rows, gate_weight, up_weight):
    gate_value = jnp.einsum("semd,edf->semf", rows, gate_weight, preferred_element_type=jnp.float32)
    up_value = jnp.einsum("semd,edf->semf", rows, up_weight, preferred_element_type=jnp.float32)
    return (gate_value, up_value)


def local_backward(gate_value, up_value, grad_rows, down_weight):
    silu_gate = jax.nn.silu(gate_value)
    sigmoid_gate = jax.nn.sigmoid(gate_value)
    hidden = (silu_gate * up_value).astype(jnp.bfloat16)
    hidden_grad = jnp.einsum(
        "semd,efd->semf", grad_rows, down_weight, preferred_element_type=jnp.float32
    )
    up_grad = (hidden_grad * silu_gate).astype(jnp.bfloat16)
    gate_grad = (
        hidden_grad * up_value * sigmoid_gate * (1.0 + gate_value * (1.0 - sigmoid_gate))
    ).astype(jnp.bfloat16)
    return (hidden, gate_grad, up_grad)


def weight_terms(saved_rows, grad_rows, back_hidden, gate_grad, up_grad):
    gate_term = jnp.einsum(
        "semd,semf->edf", saved_rows, gate_grad, preferred_element_type=jnp.float32
    )
    up_term = jnp.einsum("semd,semf->edf", saved_rows, up_grad, preferred_element_type=jnp.float32)
    down_term = jnp.einsum(
        "semf,semd->efd", back_hidden, grad_rows, preferred_element_type=jnp.float32
    )
    return (gate_term, up_term, down_term)


def mix_rows(base, returned, positions, weights, choices_per):
    width = returned.shape[-1]
    picked = (
        returned.reshape(-1, width)[positions].reshape(-1, choices_per, width).astype(jnp.float32)
    )
    return (base.astype(jnp.float32) + jnp.sum(weights[:, :, None] * picked, 1)).astype(
        jnp.bfloat16
    )


def local(
    fwd_in, fwd_routes, fwd_numer, bwd_saved, bwd_routes, bwd_numer, bwd_grad, w_gate, w_up, w_down
):
    groups = lax.axis_size("expert")
    inputs = fwd_in[0]
    saved = bwd_saved[0]
    grad_in = bwd_grad[0]
    model_width = inputs.shape[-1]
    half = model_width // lax.axis_size("dp")
    mine = lax.axis_index("dp") * half
    theirs = half - mine
    choices_per = fwd_routes.shape[-1]
    gate_half = w_gate[0]
    up_half = w_up[0]
    down_half = w_down[0]

    fwd_flat, fwd_rank = slot_ranks(fwd_routes[0])
    back_flat, back_rank = slot_ranks(bwd_routes[0])
    back_positions = back_flat * MOST + back_rank
    mixing = combine_weights(fwd_numer[0])
    back_mixing = combine_weights(bwd_numer[0])
    unit_weights = jnp.ones_like(back_mixing)
    back_table = slot_table(back_positions, choices_per)
    send_saved = packed_rows(saved, back_table)
    send_grad = packed_rows(grad_in, back_table, back_mixing)
    (recv_saved, recv_grad), (gate_other, up_other, down_other) = exchange(
        (send_saved, send_grad), (gate_half[0], up_half[0], down_half[0]), 0
    )
    recv_saved, recv_grad = (x.reshape(groups, 1, MOST, model_width) for x in (recv_saved, recv_grad))
    gate_full = jnp.concatenate([gate_half[0], gate_other], 1)
    up_full = jnp.concatenate([up_half[0], up_other], 1)
    down_full = jnp.concatenate([down_half[0], down_other], 0)
    gate_mine = lax.dynamic_slice_in_dim(gate_full, mine, half, 0)[None]
    up_mine = lax.dynamic_slice_in_dim(up_full, mine, half, 0)[None]

    share = MOST // 2
    side = lax.axis_index("dp")
    fwd_mine = (fwd_rank >= share).astype(jnp.int32) == side
    fwd_local = jnp.where(fwd_mine, fwd_flat * share + fwd_rank - side * share, -1)
    fwd_table = slot_table(fwd_local, choices_per, share)
    send_inputs = packed_rows(inputs, fwd_table, depth=share)
    recv_inputs = lax.all_to_all(send_inputs, "expert", split_axis=0, concat_axis=0, tiled=True)
    gate_value = jnp.einsum("smd,df->smf", recv_inputs, gate_full, preferred_element_type=jnp.float32)
    up_value = jnp.einsum("smd,df->smf", recv_inputs, up_full, preferred_element_type=jnp.float32)
    hidden = (jax.nn.silu(gate_value) * up_value).astype(jnp.bfloat16)
    out_rows = jnp.einsum(
        "smf,fd->smd", hidden, down_full, preferred_element_type=jnp.float32
    ).astype(jnp.bfloat16)

    back_gate, back_up = project(recv_saved, gate_half, up_half)
    back_hidden, gate_grad, up_grad = local_backward(back_gate, back_up, recv_grad, down_half)
    gate_term, up_term, down_term = weight_terms(
        recv_saved, recv_grad, back_hidden, gate_grad, up_grad
    )
    gate_swap, up_swap = swapped((gate_grad, up_grad))
    gate_all = jnp.concatenate([gate_grad, gate_swap], -1)
    up_all = jnp.concatenate([up_grad, up_swap], -1)
    grad_part = (
        jnp.einsum("semf,edf->semd", gate_all, gate_mine, preferred_element_type=jnp.float32)
        + jnp.einsum("semf,edf->semd", up_all, up_mine, preferred_element_type=jnp.float32)
    ).astype(jnp.bfloat16)

    back_out = lax.all_to_all(out_rows, "expert", split_axis=0, concat_axis=0, tiled=True)
    picked = back_out.reshape(-1, model_width)[jnp.maximum(fwd_local, 0)].reshape(-1, choices_per, model_width)
    weights = jnp.where(fwd_mine, mixing.reshape(-1), 0.0).reshape(-1, choices_per)
    partial = jnp.sum(weights[:, :, None] * picked.astype(jnp.float32), 1)
    partial_other = swapped(partial)
    first = side == 0
    layer_out = (
        (inputs.astype(jnp.float32) + jnp.where(first, partial, partial_other))
        + jnp.where(first, partial_other, partial)
    ).astype(jnp.bfloat16)
    next_fwd = passed_along(layer_out, "section", 1)[None]

    back_grad = lax.all_to_all(grad_part, "expert", split_axis=0, concat_axis=0, tiled=True)
    grad_in_part = lax.dynamic_slice_in_dim(grad_in, mine, half, 1)
    input_grad = mix_rows(grad_in_part, back_grad, back_positions, unit_weights, choices_per)
    next_bwd = handoff(input_grad, -1)[None]
    gate_sum = gate_term.astype(jnp.bfloat16)
    up_sum = up_term.astype(jnp.bfloat16)
    down_sum = down_term.astype(jnp.bfloat16)
    return (next_fwd, next_bwd, gate_sum[None], up_sum[None], down_sum[None])


def solution(mesh):
    in_specs = (
        P("section", "expert", None),
        P("section", "expert", None),
        P("section", "expert", None),
        P("section", "expert", None),
        P("section", "expert", None),
        P("section", "expert", None),
        P("section", "expert", None),
        P("section", "expert", None, "dp"),
        P("section", "expert", None, "dp"),
        P("section", "expert", "dp", None),
    )
    out_specs = (
        P("section", "expert", None),
        P("section", "expert", None),
        P("section", "expert", None, "dp"),
        P("section", "expert", None, "dp"),
        P("section", "expert", "dp", None),
    )
    return jax.shard_map(local, mesh=mesh, in_specs=in_specs, out_specs=out_specs, check_vma=False)
```

```python
import functools

import jax
import jax.numpy as jnp
from jax import lax
from jax.experimental import pallas as pl
from jax.experimental.pallas import tpu as pltpu
from jax.sharding import PartitionSpec as P

MESH = pl.DeviceIdType.MESH

EXPERTS = 32
MOST = 26


def passed_along(block, axis, distance):
    devices = range(lax.axis_size(axis))
    route = [((i - distance) % len(devices), i) for i in devices]
    return lax.ppermute(block, axis, route)


def swapped(block):
    return lax.ppermute(block, "dp", [(0, 1), (1, 0)])


def exchange_kernel(n, spread, swapped_count, *refs):
    sends = refs[0:spread]
    swaps_out = refs[spread:spread + swapped_count]
    recvs = refs[spread + swapped_count:2 * spread + swapped_count]
    swaps_in = refs[2 * spread + swapped_count:2 * (spread + swapped_count)]
    send_sems, recv_sems, w_send, w_recv, local_sems = refs[2 * (spread + swapped_count):]
    me = lax.axis_index("expert")
    other = 1 - lax.axis_index("dp")

    barrier = pltpu.get_barrier_semaphore()

    def greet(o, carry):
        pl.semaphore_signal(barrier, 1, device_id={"expert": lax.rem(me + o, n)}, device_id_type=MESH)
        return carry

    lax.fori_loop(1, n, greet, 0)
    if swapped_count:
        pl.semaphore_signal(barrier, 1, device_id={"dp": other}, device_id_type=MESH)
    pl.semaphore_wait(barrier, n if swapped_count else n - 1)

    def copy_of(a, o):
        target = lax.rem(me + o, n)
        return pltpu.make_async_remote_copy(
            src_ref=sends[a].at[target],
            dst_ref=recvs[a].at[me],
            send_sem=send_sems.at[a, o],
            recv_sem=recv_sems.at[a, o],
            device_id={"expert": target},
            device_id_type=MESH,
        )

    swaps = [
        pltpu.make_async_remote_copy(
            src_ref=swaps_out[i],
            dst_ref=swaps_in[i],
            send_sem=w_send.at[i],
            recv_sem=w_recv.at[i],
            device_id={"dp": other},
            device_id_type=MESH,
        )
        for i in range(swapped_count)
    ]
    for swap in swaps:
        swap.start()
    locals_ = [
        pltpu.make_async_copy(sends[a].at[me], recvs[a].at[me], local_sems.at[a]) for a in range(spread)
    ]
    for a in range(spread):
        locals_[a].start()

        def start(o, carry, a=a):
            copy_of(a, o).start()
            return carry

        lax.fori_loop(1, n, start, 0)
    for a in range(spread):

        def finish(o, carry, a=a):
            copy_of(a, o).wait()
            return carry

        lax.fori_loop(1, n, finish, 0)
        locals_[a].wait()
    for swap in swaps:
        swap.wait()


def exchange(sends, swaps_out, collective_id):
    n = sends[0].shape[0]
    anywhere = pl.BlockSpec(memory_space=pl.ANY)
    arrays = (*sends, *swaps_out)
    moved = sum(x.size * x.dtype.itemsize for x in arrays)
    outs = pl.pallas_call(
        functools.partial(exchange_kernel, n, len(sends), len(swaps_out)),
        out_shape=[jax.ShapeDtypeStruct(x.shape, x.dtype) for x in arrays],
        in_specs=[anywhere] * len(arrays),
        out_specs=[anywhere] * len(arrays),
        scratch_shapes=[
            pltpu.SemaphoreType.DMA((len(sends), n)),
            pltpu.SemaphoreType.DMA((len(sends), n)),
            pltpu.SemaphoreType.DMA((max(1, len(swaps_out)),)),
            pltpu.SemaphoreType.DMA((max(1, len(swaps_out)),)),
            pltpu.SemaphoreType.DMA((len(sends),)),
        ],
        compiler_params=pltpu.CompilerParams(collective_id=collective_id, has_side_effects=True),
        cost_estimate=pl.CostEstimate(flops=0, bytes_accessed=2 * moved, transcendentals=0),
    )(*arrays)
    return outs[: len(sends)], outs[len(sends):]


def slot_ranks(routes):
    flat_routes = routes.reshape(-1)
    onehot_table = (flat_routes[:, None] == jnp.arange(EXPERTS, dtype=jnp.int32)[None, :]).astype(
        jnp.int32
    )
    earlier = jnp.cumsum(onehot_table, 0) - onehot_table
    return (flat_routes, jnp.sum(earlier * onehot_table, 1))


def combine_weights(numerators):
    counted = numerators.astype(jnp.float32)
    return counted / jnp.sum(counted, -1, keepdims=True)


def slot_table(positions, choices_per, depth=MOST):
    slots = jnp.arange(EXPERTS * depth, dtype=jnp.int32)
    return slots[:, None, None] == positions.reshape(-1, choices_per)[None, :, :]


def packed_rows(rows, table, scale=None, depth=MOST):
    chosen = jnp.any(table, -1).reshape(EXPERTS, depth, -1)
    picked = jnp.einsum("ecm,md->ecd", chosen.astype(rows.dtype), rows, preferred_element_type=jnp.float32)
    if scale is not None:
        picked = picked * jnp.sum(jnp.where(table, scale[None], 0.0), (1, 2)).reshape(EXPERTS, depth, 1)
    return picked.astype(rows.dtype)


def handoff(value, direction):
    sections = lax.axis_size("section")
    same = passed_along(value, "section", direction)
    route = [(i * 2 + j, ((i + direction) % sections) * 2 + 1 - j) for i in range(sections) for j in range(2)]
    crossed = lax.ppermute(value, ("section", "dp"), route)
    first = lax.axis_index("dp") == 0
    return jnp.concatenate([jnp.where(first, same, crossed), jnp.where(first, crossed, same)], 1)


def project(rows, gate_weight, up_weight):
    gate_value = jnp.einsum("semd,edf->semf", rows, gate_weight, preferred_element_type=jnp.float32)
    up_value = jnp.einsum("semd,edf->semf", rows, up_weight, preferred_element_type=jnp.float32)
    return (gate_value, up_value)


def local_backward(gate_value, up_value, grad_rows, down_weight):
    silu_gate = jax.nn.silu(gate_value)
    sigmoid_gate = jax.nn.sigmoid(gate_value)
    hidden = (silu_gate * up_value).astype(jnp.bfloat16)
    hidden_grad = jnp.einsum(
        "semd,efd->semf", grad_rows, down_weight, preferred_element_type=jnp.float32
    )
    up_grad = (hidden_grad * silu_gate).astype(jnp.bfloat16)
    gate_grad = (
        hidden_grad * up_value * sigmoid_gate * (1.0 + gate_value * (1.0 - sigmoid_gate))
    ).astype(jnp.bfloat16)
    return (hidden, gate_grad, up_grad)


def weight_terms(saved_rows, grad_rows, back_hidden, gate_grad, up_grad):
    gate_term = jnp.einsum(
        "semd,semf->edf", saved_rows, gate_grad, preferred_element_type=jnp.float32
    )
    up_term = jnp.einsum("semd,semf->edf", saved_rows, up_grad, preferred_element_type=jnp.float32)
    down_term = jnp.einsum(
        "semf,semd->efd", back_hidden, grad_rows, preferred_element_type=jnp.float32
    )
    return (gate_term, up_term, down_term)


def mix_rows(base, returned, positions, weights, choices_per):
    width = returned.shape[-1]
    picked = (
        returned.reshape(-1, width)[positions].reshape(-1, choices_per, width).astype(jnp.float32)
    )
    return (base.astype(jnp.float32) + jnp.sum(weights[:, :, None] * picked, 1)).astype(
        jnp.bfloat16
    )


def local(
    fwd_in, fwd_routes, fwd_numer, bwd_saved, bwd_routes, bwd_numer, bwd_grad, w_gate, w_up, w_down
):
    groups = lax.axis_size("expert")
    inputs = fwd_in[0]
    saved = bwd_saved[0]
    grad_in = bwd_grad[0]
    model_width = inputs.shape[-1]
    half = model_width // lax.axis_size("dp")
    mine = lax.axis_index("dp") * half
    theirs = half - mine
    choices_per = fwd_routes.shape[-1]
    gate_half = w_gate[0]
    up_half = w_up[0]
    down_half = w_down[0]

    fwd_flat, fwd_rank = slot_ranks(fwd_routes[0])
    back_flat, back_rank = slot_ranks(bwd_routes[0])
    back_positions = back_flat * MOST + back_rank
    mixing = combine_weights(fwd_numer[0])
    back_mixing = combine_weights(bwd_numer[0])
    unit_weights = jnp.ones_like(back_mixing)
    back_table = slot_table(back_positions, choices_per)
    send_saved = packed_rows(saved, back_table)
    send_grad = packed_rows(grad_in, back_table, back_mixing)
    (recv_saved, recv_grad), (gate_other, up_other, down_other) = exchange(
        (send_saved, send_grad), (gate_half[0], up_half[0], down_half[0]), 0
    )
    recv_saved, recv_grad = (x.reshape(groups, 1, MOST, model_width) for x in (recv_saved, recv_grad))
    gate_full = jnp.concatenate([gate_half[0], gate_other], 1)
    up_full = jnp.concatenate([up_half[0], up_other], 1)
    down_full = jnp.concatenate([down_half[0], down_other], 0)

    share = MOST // 2
    side = lax.axis_index("dp")
    fwd_mine = (fwd_rank >= share).astype(jnp.int32) == side
    fwd_local = jnp.where(fwd_mine, fwd_flat * share + fwd_rank - side * share, -1)
    fwd_table = slot_table(fwd_local, choices_per, share)
    send_inputs = packed_rows(inputs, fwd_table, depth=share)
    recv_inputs = lax.all_to_all(send_inputs, "expert", split_axis=0, concat_axis=0, tiled=True)
    gate_value = jnp.einsum("smd,df->smf", recv_inputs, gate_full, preferred_element_type=jnp.float32)
    up_value = jnp.einsum("smd,df->smf", recv_inputs, up_full, preferred_element_type=jnp.float32)
    hidden = (jax.nn.silu(gate_value) * up_value).astype(jnp.bfloat16)
    out_rows = jnp.einsum(
        "smf,fd->smd", hidden, down_full, preferred_element_type=jnp.float32
    ).astype(jnp.bfloat16)

    back_gate, back_up = project(recv_saved, gate_half, up_half)
    back_hidden, gate_grad, up_grad = local_backward(back_gate, back_up, recv_grad, down_half)
    gate_term, up_term, down_term = weight_terms(
        recv_saved, recv_grad, back_hidden, gate_grad, up_grad
    )
    saved_share = lax.dynamic_slice_in_dim(recv_saved[:, 0], side * share, share, 1)
    grad_share = lax.dynamic_slice_in_dim(recv_grad[:, 0], side * share, share, 1)
    other_gate = jnp.einsum("smd,df->smf", saved_share, gate_other, preferred_element_type=jnp.float32)
    other_up = jnp.einsum("smd,df->smf", saved_share, up_other, preferred_element_type=jnp.float32)
    _, other_gate_grad, other_up_grad = local_backward(
        other_gate[:, None], other_up[:, None], grad_share[:, None], down_other[None]
    )
    gate_share = jnp.concatenate(
        [lax.dynamic_slice_in_dim(gate_grad[:, 0], side * share, share, 1), other_gate_grad[:, 0]], -1
    )
    up_share = jnp.concatenate(
        [lax.dynamic_slice_in_dim(up_grad[:, 0], side * share, share, 1), other_up_grad[:, 0]], -1
    )
    grad_rows = (
        jnp.einsum("smf,df->smd", gate_share, gate_full, preferred_element_type=jnp.float32)
        + jnp.einsum("smf,df->smd", up_share, up_full, preferred_element_type=jnp.float32)
    ).astype(jnp.bfloat16)

    back_out = lax.all_to_all(out_rows, "expert", split_axis=0, concat_axis=0, tiled=True)
    picked = back_out.reshape(-1, model_width)[jnp.maximum(fwd_local, 0)].reshape(-1, choices_per, model_width)
    weights = jnp.where(fwd_mine, mixing.reshape(-1), 0.0).reshape(-1, choices_per)
    partial = jnp.sum(weights[:, :, None] * picked.astype(jnp.float32), 1)

    back_grad = lax.all_to_all(grad_rows, "expert", split_axis=0, concat_axis=0, tiled=True)
    back_mine = (back_rank >= share).astype(jnp.int32) == side
    back_local = jnp.where(back_mine, back_flat * share + back_rank - side * share, 0)
    picked_grad = back_grad.reshape(-1, model_width)[back_local].reshape(-1, choices_per, model_width)
    grad_partial = jnp.sum(
        jnp.where(back_mine.reshape(-1, choices_per)[:, :, None], picked_grad.astype(jnp.float32), 0.0), 1
    )
    partial_other, grad_partial_other = swapped((partial, grad_partial))
    first = side == 0
    layer_out = (
        (inputs.astype(jnp.float32) + jnp.where(first, partial, partial_other))
        + jnp.where(first, partial_other, partial)
    ).astype(jnp.bfloat16)
    input_grad = (
        (grad_in.astype(jnp.float32) + jnp.where(first, grad_partial, grad_partial_other))
        + jnp.where(first, grad_partial_other, grad_partial)
    ).astype(jnp.bfloat16)
    next_fwd = passed_along(layer_out, "section", 1)[None]
    next_bwd = passed_along(input_grad, "section", -1)[None]
    gate_sum = gate_term.astype(jnp.bfloat16)
    up_sum = up_term.astype(jnp.bfloat16)
    down_sum = down_term.astype(jnp.bfloat16)
    return (next_fwd, next_bwd, gate_sum[None], up_sum[None], down_sum[None])


def solution(mesh):
    in_specs = (
        P("section", "expert", None),
        P("section", "expert", None),
        P("section", "expert", None),
        P("section", "expert", None),
        P("section", "expert", None),
        P("section", "expert", None),
        P("section", "expert", None),
        P("section", "expert", None, "dp"),
        P("section", "expert", None, "dp"),
        P("section", "expert", "dp", None),
    )
    out_specs = (
        P("section", "expert", None),
        P("section", "expert", None),
        P("section", "expert", None, "dp"),
        P("section", "expert", None, "dp"),
        P("section", "expert", "dp", None),
    )
    return jax.shard_map(local, mesh=mesh, in_specs=in_specs, out_specs=out_specs, check_vma=False)
```

```python
import functools

import jax
import jax.numpy as jnp
from jax import lax
from jax.experimental import pallas as pl
from jax.experimental.pallas import tpu as pltpu
from jax.sharding import PartitionSpec as P

MESH = pl.DeviceIdType.MESH

EXPERTS = 32
MOST = 26


def passed_along(block, axis, distance):
    devices = range(lax.axis_size(axis))
    route = [((i - distance) % len(devices), i) for i in devices]
    return lax.ppermute(block, axis, route)


def swapped(block):
    return lax.ppermute(block, "dp", [(0, 1), (1, 0)])


def exchange_kernel(n, spread, swapped_count, *refs):
    sends = refs[0:spread]
    swaps_out = refs[spread:spread + swapped_count]
    recvs = refs[spread + swapped_count:2 * spread + swapped_count]
    swaps_in = refs[2 * spread + swapped_count:2 * (spread + swapped_count)]
    send_sems, recv_sems, w_send, w_recv, local_sems = refs[2 * (spread + swapped_count):]
    me = lax.axis_index("expert")
    other = 1 - lax.axis_index("dp")

    barrier = pltpu.get_barrier_semaphore()

    def greet(o, carry):
        pl.semaphore_signal(barrier, 1, device_id={"expert": lax.rem(me + o, n)}, device_id_type=MESH)
        return carry

    lax.fori_loop(1, n, greet, 0)
    if swapped_count:
        pl.semaphore_signal(barrier, 1, device_id={"dp": other}, device_id_type=MESH)
    pl.semaphore_wait(barrier, n if swapped_count else n - 1)

    def copy_of(a, o):
        target = lax.rem(me + o, n)
        return pltpu.make_async_remote_copy(
            src_ref=sends[a].at[target],
            dst_ref=recvs[a].at[me],
            send_sem=send_sems.at[a, o],
            recv_sem=recv_sems.at[a, o],
            device_id={"expert": target},
            device_id_type=MESH,
        )

    swaps = [
        pltpu.make_async_remote_copy(
            src_ref=swaps_out[i],
            dst_ref=swaps_in[i],
            send_sem=w_send.at[i],
            recv_sem=w_recv.at[i],
            device_id={"dp": other},
            device_id_type=MESH,
        )
        for i in range(swapped_count)
    ]
    for swap in swaps:
        swap.start()
    locals_ = [
        pltpu.make_async_copy(sends[a].at[me], recvs[a].at[me], local_sems.at[a]) for a in range(spread)
    ]
    for a in range(spread):
        locals_[a].start()

        def start(o, carry, a=a):
            copy_of(a, o).start()
            return carry

        lax.fori_loop(1, n, start, 0)
    for a in range(spread):

        def finish(o, carry, a=a):
            copy_of(a, o).wait()
            return carry

        lax.fori_loop(1, n, finish, 0)
        locals_[a].wait()
    for swap in swaps:
        swap.wait()


def exchange(sends, swaps_out, collective_id):
    n = sends[0].shape[0]
    anywhere = pl.BlockSpec(memory_space=pl.ANY)
    arrays = (*sends, *swaps_out)
    moved = sum(x.size * x.dtype.itemsize for x in arrays)
    outs = pl.pallas_call(
        functools.partial(exchange_kernel, n, len(sends), len(swaps_out)),
        out_shape=[jax.ShapeDtypeStruct(x.shape, x.dtype) for x in arrays],
        in_specs=[anywhere] * len(arrays),
        out_specs=[anywhere] * len(arrays),
        scratch_shapes=[
            pltpu.SemaphoreType.DMA((len(sends), n)),
            pltpu.SemaphoreType.DMA((len(sends), n)),
            pltpu.SemaphoreType.DMA((max(1, len(swaps_out)),)),
            pltpu.SemaphoreType.DMA((max(1, len(swaps_out)),)),
            pltpu.SemaphoreType.DMA((len(sends),)),
        ],
        compiler_params=pltpu.CompilerParams(collective_id=collective_id, has_side_effects=True),
        cost_estimate=pl.CostEstimate(flops=0, bytes_accessed=2 * moved, transcendentals=0),
    )(*arrays)
    return outs[: len(sends)], outs[len(sends):]


def slot_ranks(routes):
    flat_routes = routes.reshape(-1)
    onehot_table = (flat_routes[:, None] == jnp.arange(EXPERTS, dtype=jnp.int32)[None, :]).astype(
        jnp.int32
    )
    earlier = jnp.cumsum(onehot_table, 0) - onehot_table
    return (flat_routes, jnp.sum(earlier * onehot_table, 1))


def combine_weights(numerators):
    counted = numerators.astype(jnp.float32)
    return counted / jnp.sum(counted, -1, keepdims=True)


def slot_table(positions, choices_per, depth=MOST):
    slots = jnp.arange(EXPERTS * depth, dtype=jnp.int32)
    return slots[:, None, None] == positions.reshape(-1, choices_per)[None, :, :]


def packed_rows(rows, table, scale=None, depth=MOST):
    chosen = jnp.any(table, -1).reshape(EXPERTS, depth, -1)
    picked = jnp.einsum("ecm,md->ecd", chosen.astype(rows.dtype), rows, preferred_element_type=jnp.float32)
    if scale is not None:
        picked = picked * jnp.sum(jnp.where(table, scale[None], 0.0), (1, 2)).reshape(EXPERTS, depth, 1)
    return picked.astype(rows.dtype)


def handoff(value, direction):
    sections = lax.axis_size("section")
    same = passed_along(value, "section", direction)
    route = [(i * 2 + j, ((i + direction) % sections) * 2 + 1 - j) for i in range(sections) for j in range(2)]
    crossed = lax.ppermute(value, ("section", "dp"), route)
    first = lax.axis_index("dp") == 0
    return jnp.concatenate([jnp.where(first, same, crossed), jnp.where(first, crossed, same)], 1)


def project(rows, gate_weight, up_weight):
    gate_value = jnp.einsum("semd,edf->semf", rows, gate_weight, preferred_element_type=jnp.float32)
    up_value = jnp.einsum("semd,edf->semf", rows, up_weight, preferred_element_type=jnp.float32)
    return (gate_value, up_value)


def local_backward(gate_value, up_value, grad_rows, down_weight):
    silu_gate = jax.nn.silu(gate_value)
    sigmoid_gate = jax.nn.sigmoid(gate_value)
    hidden = (silu_gate * up_value).astype(jnp.bfloat16)
    hidden_grad = jnp.einsum(
        "semd,efd->semf", grad_rows, down_weight, preferred_element_type=jnp.float32
    )
    up_grad = (hidden_grad * silu_gate).astype(jnp.bfloat16)
    gate_grad = (
        hidden_grad * up_value * sigmoid_gate * (1.0 + gate_value * (1.0 - sigmoid_gate))
    ).astype(jnp.bfloat16)
    return (hidden, gate_grad, up_grad)


def weight_terms(saved_rows, grad_rows, back_hidden, gate_grad, up_grad):
    gate_term = jnp.einsum(
        "semd,semf->edf", saved_rows, gate_grad, preferred_element_type=jnp.float32
    )
    up_term = jnp.einsum("semd,semf->edf", saved_rows, up_grad, preferred_element_type=jnp.float32)
    down_term = jnp.einsum(
        "semf,semd->efd", back_hidden, grad_rows, preferred_element_type=jnp.float32
    )
    return (gate_term, up_term, down_term)


def mix_rows(base, returned, positions, weights, choices_per):
    width = returned.shape[-1]
    picked = (
        returned.reshape(-1, width)[positions].reshape(-1, choices_per, width).astype(jnp.float32)
    )
    return (base.astype(jnp.float32) + jnp.sum(weights[:, :, None] * picked, 1)).astype(
        jnp.bfloat16
    )


def local(
    fwd_in, fwd_routes, fwd_numer, bwd_saved, bwd_routes, bwd_numer, bwd_grad, w_gate, w_up, w_down
):
    groups = lax.axis_size("expert")
    inputs = fwd_in[0]
    saved = bwd_saved[0]
    grad_in = bwd_grad[0]
    model_width = inputs.shape[-1]
    half = model_width // lax.axis_size("dp")
    mine = lax.axis_index("dp") * half
    theirs = half - mine
    choices_per = fwd_routes.shape[-1]
    gate_half = w_gate[0]
    up_half = w_up[0]
    down_half = w_down[0]

    fwd_flat, fwd_rank = slot_ranks(fwd_routes[0])
    back_flat, back_rank = slot_ranks(bwd_routes[0])
    back_positions = back_flat * MOST + back_rank
    mixing = combine_weights(fwd_numer[0])
    back_mixing = combine_weights(bwd_numer[0])
    unit_weights = jnp.ones_like(back_mixing)
    back_table = slot_table(back_positions, choices_per)
    send_saved = packed_rows(saved, back_table)
    send_grad = packed_rows(grad_in, back_table, back_mixing)
    (recv_saved, recv_grad), (gate_other, up_other, down_other) = exchange(
        (send_saved, send_grad), (gate_half[0], up_half[0], down_half[0]), 0
    )
    recv_saved, recv_grad = (x.reshape(groups, 1, MOST, model_width) for x in (recv_saved, recv_grad))
    gate_full = jnp.concatenate([gate_half[0], gate_other], 1)
    up_full = jnp.concatenate([up_half[0], up_other], 1)
    down_full = jnp.concatenate([down_half[0], down_other], 0)

    share = MOST // 2
    side = lax.axis_index("dp")
    fwd_mine = (fwd_rank >= share).astype(jnp.int32) == side
    fwd_local = jnp.where(fwd_mine, fwd_flat * share + fwd_rank - side * share, -1)
    fwd_table = slot_table(fwd_local, choices_per, share)
    send_inputs = packed_rows(inputs, fwd_table, depth=share)
    recv_inputs = lax.all_to_all(send_inputs, "expert", split_axis=0, concat_axis=0, tiled=True)
    gate_value = jnp.einsum("smd,df->smf", recv_inputs, gate_full, preferred_element_type=jnp.float32)
    up_value = jnp.einsum("smd,df->smf", recv_inputs, up_full, preferred_element_type=jnp.float32)
    hidden = (jax.nn.silu(gate_value) * up_value).astype(jnp.bfloat16)
    out_rows = jnp.einsum(
        "smf,fd->smd", hidden, down_full, preferred_element_type=jnp.float32
    ).astype(jnp.bfloat16)

    out_rows, recv_saved, recv_grad = lax.optimization_barrier((out_rows, recv_saved, recv_grad))
    back_out = lax.all_to_all(out_rows, "expert", split_axis=0, concat_axis=0, tiled=True)
    back_gate, back_up = project(recv_saved, gate_half, up_half)
    back_hidden, gate_grad, up_grad = local_backward(back_gate, back_up, recv_grad, down_half)
    gate_term, up_term, down_term = weight_terms(
        recv_saved, recv_grad, back_hidden, gate_grad, up_grad
    )
    saved_share = lax.dynamic_slice_in_dim(recv_saved[:, 0], side * share, share, 1)
    grad_share = lax.dynamic_slice_in_dim(recv_grad[:, 0], side * share, share, 1)
    other_gate = jnp.einsum("smd,df->smf", saved_share, gate_other, preferred_element_type=jnp.float32)
    other_up = jnp.einsum("smd,df->smf", saved_share, up_other, preferred_element_type=jnp.float32)
    _, other_gate_grad, other_up_grad = local_backward(
        other_gate[:, None], other_up[:, None], grad_share[:, None], down_other[None]
    )
    gate_share = jnp.concatenate(
        [lax.dynamic_slice_in_dim(gate_grad[:, 0], side * share, share, 1), other_gate_grad[:, 0]], -1
    )
    up_share = jnp.concatenate(
        [lax.dynamic_slice_in_dim(up_grad[:, 0], side * share, share, 1), other_up_grad[:, 0]], -1
    )
    grad_rows = (
        jnp.einsum("smf,df->smd", gate_share, gate_full, preferred_element_type=jnp.float32)
        + jnp.einsum("smf,df->smd", up_share, up_full, preferred_element_type=jnp.float32)
    ).astype(jnp.bfloat16)

    picked = back_out.reshape(-1, model_width)[jnp.maximum(fwd_local, 0)].reshape(-1, choices_per, model_width)
    weights = jnp.where(fwd_mine, mixing.reshape(-1), 0.0).reshape(-1, choices_per)
    partial = jnp.sum(weights[:, :, None] * picked.astype(jnp.float32), 1)

    back_grad = lax.all_to_all(grad_rows, "expert", split_axis=0, concat_axis=0, tiled=True)
    back_mine = (back_rank >= share).astype(jnp.int32) == side
    back_local = jnp.where(back_mine, back_flat * share + back_rank - side * share, 0)
    picked_grad = back_grad.reshape(-1, model_width)[back_local].reshape(-1, choices_per, model_width)
    grad_partial = jnp.sum(
        jnp.where(back_mine.reshape(-1, choices_per)[:, :, None], picked_grad.astype(jnp.float32), 0.0), 1
    )
    partial_other, grad_partial_other = swapped((partial, grad_partial))
    first = side == 0
    layer_out = (
        (inputs.astype(jnp.float32) + jnp.where(first, partial, partial_other))
        + jnp.where(first, partial_other, partial)
    ).astype(jnp.bfloat16)
    input_grad = (
        (grad_in.astype(jnp.float32) + jnp.where(first, grad_partial, grad_partial_other))
        + jnp.where(first, grad_partial_other, grad_partial)
    ).astype(jnp.bfloat16)
    next_fwd = passed_along(layer_out, "section", 1)[None]
    next_bwd = passed_along(input_grad, "section", -1)[None]
    gate_sum = gate_term.astype(jnp.bfloat16)
    up_sum = up_term.astype(jnp.bfloat16)
    down_sum = down_term.astype(jnp.bfloat16)
    return (next_fwd, next_bwd, gate_sum[None], up_sum[None], down_sum[None])


def solution(mesh):
    in_specs = (
        P("section", "expert", None),
        P("section", "expert", None),
        P("section", "expert", None),
        P("section", "expert", None),
        P("section", "expert", None),
        P("section", "expert", None),
        P("section", "expert", None),
        P("section", "expert", None, "dp"),
        P("section", "expert", None, "dp"),
        P("section", "expert", "dp", None),
    )
    out_specs = (
        P("section", "expert", None),
        P("section", "expert", None),
        P("section", "expert", None, "dp"),
        P("section", "expert", None, "dp"),
        P("section", "expert", "dp", None),
    )
    return jax.shard_map(local, mesh=mesh, in_specs=in_specs, out_specs=out_specs, check_vma=False)
```

```python
import functools

import jax
import jax.numpy as jnp
from jax import lax
from jax.experimental import pallas as pl
from jax.experimental.pallas import tpu as pltpu
from jax.sharding import PartitionSpec as P

MESH = pl.DeviceIdType.MESH

EXPERTS = 32
MOST = 26


def passed_along(block, axis, distance):
    devices = range(lax.axis_size(axis))
    route = [((i - distance) % len(devices), i) for i in devices]
    return lax.ppermute(block, axis, route)


def swapped(block):
    return lax.ppermute(block, "dp", [(0, 1), (1, 0)])


def exchange_kernel(n, spread, swapped_count, *refs):
    sends = refs[0:spread]
    swaps_out = refs[spread:spread + swapped_count]
    recvs = refs[spread + swapped_count:2 * spread + swapped_count]
    swaps_in = refs[2 * spread + swapped_count:2 * (spread + swapped_count)]
    send_sems, recv_sems, w_send, w_recv, local_sems = refs[2 * (spread + swapped_count):]
    me = lax.axis_index("expert")
    other = 1 - lax.axis_index("dp")

    barrier = pltpu.get_barrier_semaphore()

    def greet(o, carry):
        pl.semaphore_signal(barrier, 1, device_id={"expert": lax.rem(me + o, n)}, device_id_type=MESH)
        return carry

    lax.fori_loop(1, n, greet, 0)
    if swapped_count:
        pl.semaphore_signal(barrier, 1, device_id={"dp": other}, device_id_type=MESH)
    pl.semaphore_wait(barrier, n if swapped_count else n - 1)

    def copy_of(a, o):
        target = lax.rem(me + o, n)
        return pltpu.make_async_remote_copy(
            src_ref=sends[a].at[target],
            dst_ref=recvs[a].at[me],
            send_sem=send_sems.at[a, o],
            recv_sem=recv_sems.at[a, o],
            device_id={"expert": target},
            device_id_type=MESH,
        )

    swaps = [
        pltpu.make_async_remote_copy(
            src_ref=swaps_out[i],
            dst_ref=swaps_in[i],
            send_sem=w_send.at[i],
            recv_sem=w_recv.at[i],
            device_id={"dp": other},
            device_id_type=MESH,
        )
        for i in range(swapped_count)
    ]
    for swap in swaps:
        swap.start()
    locals_ = [
        pltpu.make_async_copy(sends[a].at[me], recvs[a].at[me], local_sems.at[a]) for a in range(spread)
    ]
    for a in range(spread):
        locals_[a].start()

        def start(o, carry, a=a):
            copy_of(a, o).start()
            return carry

        lax.fori_loop(1, n, start, 0)
    for a in range(spread):

        def finish(o, carry, a=a):
            copy_of(a, o).wait()
            return carry

        lax.fori_loop(1, n, finish, 0)
        locals_[a].wait()
    for swap in swaps:
        swap.wait()


def exchange(sends, swaps_out, collective_id):
    n = sends[0].shape[0]
    anywhere = pl.BlockSpec(memory_space=pl.ANY)
    arrays = (*sends, *swaps_out)
    moved = sum(x.size * x.dtype.itemsize for x in arrays)
    outs = pl.pallas_call(
        functools.partial(exchange_kernel, n, len(sends), len(swaps_out)),
        out_shape=[jax.ShapeDtypeStruct(x.shape, x.dtype) for x in arrays],
        in_specs=[anywhere] * len(arrays),
        out_specs=[anywhere] * len(arrays),
        scratch_shapes=[
            pltpu.SemaphoreType.DMA((len(sends), n)),
            pltpu.SemaphoreType.DMA((len(sends), n)),
            pltpu.SemaphoreType.DMA((max(1, len(swaps_out)),)),
            pltpu.SemaphoreType.DMA((max(1, len(swaps_out)),)),
            pltpu.SemaphoreType.DMA((len(sends),)),
        ],
        compiler_params=pltpu.CompilerParams(collective_id=collective_id, has_side_effects=True),
        cost_estimate=pl.CostEstimate(flops=0, bytes_accessed=2 * moved, transcendentals=0),
    )(*arrays)
    return outs[: len(sends)], outs[len(sends):]


def slot_ranks(routes):
    flat_routes = routes.reshape(-1)
    onehot_table = (flat_routes[:, None] == jnp.arange(EXPERTS, dtype=jnp.int32)[None, :]).astype(
        jnp.int32
    )
    earlier = jnp.cumsum(onehot_table, 0) - onehot_table
    return (flat_routes, jnp.sum(earlier * onehot_table, 1))


def combine_weights(numerators):
    counted = numerators.astype(jnp.float32)
    return counted / jnp.sum(counted, -1, keepdims=True)


def slot_table(positions, choices_per, depth=MOST):
    slots = jnp.arange(EXPERTS * depth, dtype=jnp.int32)
    return slots[:, None, None] == positions.reshape(-1, choices_per)[None, :, :]


def packed_rows(rows, table, scale=None, depth=MOST):
    chosen = jnp.any(table, -1).reshape(EXPERTS, depth, -1)
    picked = jnp.einsum("ecm,md->ecd", chosen.astype(rows.dtype), rows, preferred_element_type=jnp.float32)
    if scale is not None:
        picked = picked * jnp.sum(jnp.where(table, scale[None], 0.0), (1, 2)).reshape(EXPERTS, depth, 1)
    return picked.astype(rows.dtype)


def handoff(value, direction):
    sections = lax.axis_size("section")
    same = passed_along(value, "section", direction)
    route = [(i * 2 + j, ((i + direction) % sections) * 2 + 1 - j) for i in range(sections) for j in range(2)]
    crossed = lax.ppermute(value, ("section", "dp"), route)
    first = lax.axis_index("dp") == 0
    return jnp.concatenate([jnp.where(first, same, crossed), jnp.where(first, crossed, same)], 1)


def project(rows, gate_weight, up_weight):
    gate_value = jnp.einsum("semd,edf->semf", rows, gate_weight, preferred_element_type=jnp.float32)
    up_value = jnp.einsum("semd,edf->semf", rows, up_weight, preferred_element_type=jnp.float32)
    return (gate_value, up_value)


def local_backward(gate_value, up_value, grad_rows, down_weight):
    silu_gate = jax.nn.silu(gate_value)
    sigmoid_gate = jax.nn.sigmoid(gate_value)
    hidden = (silu_gate * up_value).astype(jnp.bfloat16)
    hidden_grad = jnp.einsum(
        "semd,efd->semf", grad_rows, down_weight, preferred_element_type=jnp.float32
    )
    up_grad = (hidden_grad * silu_gate).astype(jnp.bfloat16)
    gate_grad = (
        hidden_grad * up_value * sigmoid_gate * (1.0 + gate_value * (1.0 - sigmoid_gate))
    ).astype(jnp.bfloat16)
    return (hidden, gate_grad, up_grad)


def weight_terms(saved_rows, grad_rows, back_hidden, gate_grad, up_grad):
    gate_term = jnp.einsum(
        "semd,semf->edf", saved_rows, gate_grad, preferred_element_type=jnp.float32
    )
    up_term = jnp.einsum("semd,semf->edf", saved_rows, up_grad, preferred_element_type=jnp.float32)
    down_term = jnp.einsum(
        "semf,semd->efd", back_hidden, grad_rows, preferred_element_type=jnp.float32
    )
    return (gate_term, up_term, down_term)


def mix_rows(base, returned, positions, weights, choices_per):
    width = returned.shape[-1]
    picked = (
        returned.reshape(-1, width)[positions].reshape(-1, choices_per, width).astype(jnp.float32)
    )
    return (base.astype(jnp.float32) + jnp.sum(weights[:, :, None] * picked, 1)).astype(
        jnp.bfloat16
    )


def local(
    fwd_in, fwd_routes, fwd_numer, bwd_saved, bwd_routes, bwd_numer, bwd_grad, w_gate, w_up, w_down
):
    groups = lax.axis_size("expert")
    inputs = fwd_in[0]
    saved = bwd_saved[0]
    grad_in = bwd_grad[0]
    model_width = inputs.shape[-1]
    half = model_width // lax.axis_size("dp")
    mine = lax.axis_index("dp") * half
    theirs = half - mine
    choices_per = fwd_routes.shape[-1]
    gate_half = w_gate[0]
    up_half = w_up[0]
    down_half = w_down[0]

    fwd_flat, fwd_rank = slot_ranks(fwd_routes[0])
    back_flat, back_rank = slot_ranks(bwd_routes[0])
    back_positions = back_flat * MOST + back_rank
    mixing = combine_weights(fwd_numer[0])
    back_mixing = combine_weights(bwd_numer[0])
    unit_weights = jnp.ones_like(back_mixing)
    back_table = slot_table(back_positions, choices_per)
    send_saved = packed_rows(saved, back_table)
    send_grad = packed_rows(grad_in, back_table, back_mixing)
    (recv_saved, recv_grad), (gate_other, up_other, down_other) = exchange(
        (send_saved, send_grad), (gate_half[0], up_half[0], down_half[0]), 0
    )
    recv_saved, recv_grad = (x.reshape(groups, 1, MOST, model_width) for x in (recv_saved, recv_grad))
    gate_full = jnp.concatenate([gate_half[0], gate_other], 1)
    up_full = jnp.concatenate([up_half[0], up_other], 1)
    down_full = jnp.concatenate([down_half[0], down_other], 0)

    share = MOST // 2
    side = lax.axis_index("dp")
    fwd_mine = (fwd_rank >= share).astype(jnp.int32) == side
    fwd_local = jnp.where(fwd_mine, fwd_flat * share + fwd_rank - side * share, -1)
    fwd_table = slot_table(fwd_local, choices_per, share)
    send_inputs = packed_rows(inputs, fwd_table, depth=share)
    recv_inputs = lax.all_to_all(send_inputs, "expert", split_axis=0, concat_axis=0, tiled=True)
    gate_value = jnp.einsum("smd,df->smf", recv_inputs, gate_full, preferred_element_type=jnp.float32)
    up_value = jnp.einsum("smd,df->smf", recv_inputs, up_full, preferred_element_type=jnp.float32)
    hidden = (jax.nn.silu(gate_value) * up_value).astype(jnp.bfloat16)
    out_rows = jnp.einsum(
        "smf,fd->smd", hidden, down_full, preferred_element_type=jnp.float32
    ).astype(jnp.bfloat16)

    out_rows, recv_saved, recv_grad = lax.optimization_barrier((out_rows, recv_saved, recv_grad))
    back_out = lax.all_to_all(out_rows, "expert", split_axis=0, concat_axis=0, tiled=True)
    back_gate, back_up = project(recv_saved, gate_half, up_half)
    back_hidden, gate_grad, up_grad = local_backward(back_gate, back_up, recv_grad, down_half)
    gate_term, up_term, down_term = weight_terms(
        recv_saved, recv_grad, back_hidden, gate_grad, up_grad
    )
    saved_share = lax.dynamic_slice_in_dim(recv_saved[:, 0], side * share, share, 1)
    grad_share = lax.dynamic_slice_in_dim(recv_grad[:, 0], side * share, share, 1)
    other_gate = jnp.einsum("smd,df->smf", saved_share, gate_other, preferred_element_type=jnp.float32)
    other_up = jnp.einsum("smd,df->smf", saved_share, up_other, preferred_element_type=jnp.float32)
    _, other_gate_grad, other_up_grad = local_backward(
        other_gate[:, None], other_up[:, None], grad_share[:, None], down_other[None]
    )
    gate_share = jnp.concatenate(
        [lax.dynamic_slice_in_dim(gate_grad[:, 0], side * share, share, 1), other_gate_grad[:, 0]], -1
    )
    up_share = jnp.concatenate(
        [lax.dynamic_slice_in_dim(up_grad[:, 0], side * share, share, 1), other_up_grad[:, 0]], -1
    )
    grad_rows = (
        jnp.einsum("smf,df->smd", gate_share, gate_full, preferred_element_type=jnp.float32)
        + jnp.einsum("smf,df->smd", up_share, up_full, preferred_element_type=jnp.float32)
    ).astype(jnp.bfloat16)

    picked = back_out.reshape(-1, model_width)[jnp.maximum(fwd_local, 0)].reshape(-1, choices_per, model_width)
    weights = jnp.where(fwd_mine, mixing.reshape(-1), 0.0).reshape(-1, choices_per)
    partial = jnp.sum(weights[:, :, None] * picked.astype(jnp.float32), 1)
    partial_other = swapped(partial)
    first = side == 0
    layer_out = (
        (inputs.astype(jnp.float32) + jnp.where(first, partial, partial_other))
        + jnp.where(first, partial_other, partial)
    ).astype(jnp.bfloat16)
    next_fwd = passed_along(layer_out, "section", 1)[None]

    back_grad = lax.all_to_all(grad_rows, "expert", split_axis=0, concat_axis=0, tiled=True)
    back_mine = (back_rank >= share).astype(jnp.int32) == side
    back_local = jnp.where(back_mine, back_flat * share + back_rank - side * share, 0)
    picked_grad = back_grad.reshape(-1, model_width)[back_local].reshape(-1, choices_per, model_width)
    grad_partial = jnp.sum(
        jnp.where(back_mine.reshape(-1, choices_per)[:, :, None], picked_grad.astype(jnp.float32), 0.0), 1
    )
    grad_partial_other = swapped(grad_partial)
    input_grad = (
        (grad_in.astype(jnp.float32) + jnp.where(first, grad_partial, grad_partial_other))
        + jnp.where(first, grad_partial_other, grad_partial)
    ).astype(jnp.bfloat16)
    next_bwd = passed_along(input_grad, "section", -1)[None]
    gate_sum = gate_term.astype(jnp.bfloat16)
    up_sum = up_term.astype(jnp.bfloat16)
    down_sum = down_term.astype(jnp.bfloat16)
    return (next_fwd, next_bwd, gate_sum[None], up_sum[None], down_sum[None])


def solution(mesh):
    in_specs = (
        P("section", "expert", None),
        P("section", "expert", None),
        P("section", "expert", None),
        P("section", "expert", None),
        P("section", "expert", None),
        P("section", "expert", None),
        P("section", "expert", None),
        P("section", "expert", None, "dp"),
        P("section", "expert", None, "dp"),
        P("section", "expert", "dp", None),
    )
    out_specs = (
        P("section", "expert", None),
        P("section", "expert", None),
        P("section", "expert", None, "dp"),
        P("section", "expert", None, "dp"),
        P("section", "expert", "dp", None),
    )
    return jax.shard_map(local, mesh=mesh, in_specs=in_specs, out_specs=out_specs, check_vma=False)
```

```python
import functools

import jax
import jax.numpy as jnp
from jax import lax
from jax.experimental import pallas as pl
from jax.experimental.pallas import tpu as pltpu
from jax.sharding import PartitionSpec as P

MESH = pl.DeviceIdType.MESH

EXPERTS = 32
MOST = 26


def passed_along(block, axis, distance):
    devices = range(lax.axis_size(axis))
    route = [((i - distance) % len(devices), i) for i in devices]
    return lax.ppermute(block, axis, route)


def swapped(block):
    return lax.ppermute(block, "dp", [(0, 1), (1, 0)])


def exchange_kernel(n, spread, swapped_count, *refs):
    sends = refs[0:spread]
    swaps_out = refs[spread:spread + swapped_count]
    recvs = refs[spread + swapped_count:2 * spread + swapped_count]
    swaps_in = refs[2 * spread + swapped_count:2 * (spread + swapped_count)]
    send_sems, recv_sems, w_send, w_recv, local_sems = refs[2 * (spread + swapped_count):]
    me = lax.axis_index("expert")
    other = 1 - lax.axis_index("dp")

    barrier = pltpu.get_barrier_semaphore()

    def greet(o, carry):
        pl.semaphore_signal(barrier, 1, device_id={"expert": lax.rem(me + o, n)}, device_id_type=MESH)
        return carry

    lax.fori_loop(1, n, greet, 0)
    if swapped_count:
        pl.semaphore_signal(barrier, 1, device_id={"dp": other}, device_id_type=MESH)
    pl.semaphore_wait(barrier, n if swapped_count else n - 1)

    def copy_of(a, o):
        target = lax.rem(me + o, n)
        return pltpu.make_async_remote_copy(
            src_ref=sends[a].at[target],
            dst_ref=recvs[a].at[me],
            send_sem=send_sems.at[a, o],
            recv_sem=recv_sems.at[a, o],
            device_id={"expert": target},
            device_id_type=MESH,
        )

    swaps = [
        pltpu.make_async_remote_copy(
            src_ref=swaps_out[i],
            dst_ref=swaps_in[i],
            send_sem=w_send.at[i],
            recv_sem=w_recv.at[i],
            device_id={"dp": other},
            device_id_type=MESH,
        )
        for i in range(swapped_count)
    ]
    for swap in swaps:
        swap.start()
    locals_ = [
        pltpu.make_async_copy(sends[a].at[me], recvs[a].at[me], local_sems.at[a]) for a in range(spread)
    ]
    for a in range(spread):
        locals_[a].start()

        def start(o, carry, a=a):
            copy_of(a, o).start()
            return carry

        lax.fori_loop(1, n, start, 0)
    for a in range(spread):

        def finish(o, carry, a=a):
            copy_of(a, o).wait()
            return carry

        lax.fori_loop(1, n, finish, 0)
        locals_[a].wait()
    for swap in swaps:
        swap.wait()


def exchange(sends, swaps_out, collective_id):
    n = sends[0].shape[0]
    anywhere = pl.BlockSpec(memory_space=pl.ANY)
    arrays = (*sends, *swaps_out)
    moved = sum(x.size * x.dtype.itemsize for x in arrays)
    outs = pl.pallas_call(
        functools.partial(exchange_kernel, n, len(sends), len(swaps_out)),
        out_shape=[jax.ShapeDtypeStruct(x.shape, x.dtype) for x in arrays],
        in_specs=[anywhere] * len(arrays),
        out_specs=[anywhere] * len(arrays),
        scratch_shapes=[
            pltpu.SemaphoreType.DMA((len(sends), n)),
            pltpu.SemaphoreType.DMA((len(sends), n)),
            pltpu.SemaphoreType.DMA((max(1, len(swaps_out)),)),
            pltpu.SemaphoreType.DMA((max(1, len(swaps_out)),)),
            pltpu.SemaphoreType.DMA((len(sends),)),
        ],
        compiler_params=pltpu.CompilerParams(collective_id=collective_id, has_side_effects=True),
        cost_estimate=pl.CostEstimate(flops=0, bytes_accessed=2 * moved, transcendentals=0),
    )(*arrays)
    return outs[: len(sends)], outs[len(sends):]


def slot_ranks(routes):
    flat_routes = routes.reshape(-1)
    onehot_table = (flat_routes[:, None] == jnp.arange(EXPERTS, dtype=jnp.int32)[None, :]).astype(
        jnp.int32
    )
    earlier = jnp.cumsum(onehot_table, 0) - onehot_table
    return (flat_routes, jnp.sum(earlier * onehot_table, 1))


def combine_weights(numerators):
    counted = numerators.astype(jnp.float32)
    return counted / jnp.sum(counted, -1, keepdims=True)


def slot_table(positions, choices_per, depth=MOST):
    slots = jnp.arange(EXPERTS * depth, dtype=jnp.int32)
    return slots[:, None, None] == positions.reshape(-1, choices_per)[None, :, :]


def packed_rows(rows, table, scale=None, depth=MOST):
    chosen = jnp.any(table, -1).reshape(EXPERTS, depth, -1)
    picked = jnp.einsum("ecm,md->ecd", chosen.astype(rows.dtype), rows, preferred_element_type=jnp.float32)
    if scale is not None:
        picked = picked * jnp.sum(jnp.where(table, scale[None], 0.0), (1, 2)).reshape(EXPERTS, depth, 1)
    return picked.astype(rows.dtype)


def handoff(value, direction):
    sections = lax.axis_size("section")
    same = passed_along(value, "section", direction)
    route = [(i * 2 + j, ((i + direction) % sections) * 2 + 1 - j) for i in range(sections) for j in range(2)]
    crossed = lax.ppermute(value, ("section", "dp"), route)
    first = lax.axis_index("dp") == 0
    return jnp.concatenate([jnp.where(first, same, crossed), jnp.where(first, crossed, same)], 1)


def project(rows, gate_weight, up_weight):
    gate_value = jnp.einsum("semd,edf->semf", rows, gate_weight, preferred_element_type=jnp.float32)
    up_value = jnp.einsum("semd,edf->semf", rows, up_weight, preferred_element_type=jnp.float32)
    return (gate_value, up_value)


def local_backward(gate_value, up_value, grad_rows, down_weight):
    silu_gate = jax.nn.silu(gate_value)
    sigmoid_gate = jax.nn.sigmoid(gate_value)
    hidden = (silu_gate * up_value).astype(jnp.bfloat16)
    hidden_grad = jnp.einsum(
        "semd,efd->semf", grad_rows, down_weight, preferred_element_type=jnp.float32
    )
    up_grad = (hidden_grad * silu_gate).astype(jnp.bfloat16)
    gate_grad = (
        hidden_grad * up_value * sigmoid_gate * (1.0 + gate_value * (1.0 - sigmoid_gate))
    ).astype(jnp.bfloat16)
    return (hidden, gate_grad, up_grad)


def weight_terms(saved_rows, grad_rows, back_hidden, gate_grad, up_grad):
    gate_term = jnp.einsum(
        "semd,semf->edf", saved_rows, gate_grad, preferred_element_type=jnp.float32
    )
    up_term = jnp.einsum("semd,semf->edf", saved_rows, up_grad, preferred_element_type=jnp.float32)
    down_term = jnp.einsum(
        "semf,semd->efd", back_hidden, grad_rows, preferred_element_type=jnp.float32
    )
    return (gate_term, up_term, down_term)


def mix_rows(base, returned, positions, weights, choices_per):
    width = returned.shape[-1]
    picked = (
        returned.reshape(-1, width)[positions].reshape(-1, choices_per, width).astype(jnp.float32)
    )
    return (base.astype(jnp.float32) + jnp.sum(weights[:, :, None] * picked, 1)).astype(
        jnp.bfloat16
    )


def local(
    fwd_in, fwd_routes, fwd_numer, bwd_saved, bwd_routes, bwd_numer, bwd_grad, w_gate, w_up, w_down
):
    groups = lax.axis_size("expert")
    inputs = fwd_in[0]
    saved = bwd_saved[0]
    grad_in = bwd_grad[0]
    model_width = inputs.shape[-1]
    half = model_width // lax.axis_size("dp")
    mine = lax.axis_index("dp") * half
    theirs = half - mine
    choices_per = fwd_routes.shape[-1]
    gate_half = w_gate[0]
    up_half = w_up[0]
    down_half = w_down[0]

    fwd_flat, fwd_rank = slot_ranks(fwd_routes[0])
    back_flat, back_rank = slot_ranks(bwd_routes[0])
    back_positions = back_flat * MOST + back_rank
    mixing = combine_weights(fwd_numer[0])
    back_mixing = combine_weights(bwd_numer[0])
    unit_weights = jnp.ones_like(back_mixing)
    back_table = slot_table(back_positions, choices_per)
    send_saved = packed_rows(saved, back_table)
    send_grad = packed_rows(grad_in, back_table, back_mixing)
    share = MOST // 2
    side = lax.axis_index("dp")
    fwd_mine = (fwd_rank >= share).astype(jnp.int32) == side
    fwd_local = jnp.where(fwd_mine, fwd_flat * share + fwd_rank - side * share, -1)
    fwd_table = slot_table(fwd_local, choices_per, share)
    send_inputs = packed_rows(inputs, fwd_table, depth=share)
    (recv_saved, recv_grad, recv_inputs), (gate_other, up_other, down_other) = exchange(
        (send_saved, send_grad, send_inputs), (gate_half[0], up_half[0], down_half[0]), 0
    )
    recv_saved, recv_grad = (x.reshape(groups, 1, MOST, model_width) for x in (recv_saved, recv_grad))
    gate_full = jnp.concatenate([gate_half[0], gate_other], 1)
    up_full = jnp.concatenate([up_half[0], up_other], 1)
    down_full = jnp.concatenate([down_half[0], down_other], 0)
    gate_mine = lax.dynamic_slice_in_dim(gate_full, mine, half, 0)[None]
    up_mine = lax.dynamic_slice_in_dim(up_full, mine, half, 0)[None]

    gate_value = jnp.einsum("smd,df->smf", recv_inputs, gate_full, preferred_element_type=jnp.float32)
    up_value = jnp.einsum("smd,df->smf", recv_inputs, up_full, preferred_element_type=jnp.float32)
    hidden = (jax.nn.silu(gate_value) * up_value).astype(jnp.bfloat16)
    out_rows = jnp.einsum(
        "smf,fd->smd", hidden, down_full, preferred_element_type=jnp.float32
    ).astype(jnp.bfloat16)

    back_gate, back_up = project(recv_saved, gate_half, up_half)
    back_hidden, gate_grad, up_grad = local_backward(back_gate, back_up, recv_grad, down_half)
    gate_term, up_term, down_term = weight_terms(
        recv_saved, recv_grad, back_hidden, gate_grad, up_grad
    )
    gate_swap, up_swap = swapped((gate_grad, up_grad))
    gate_all = jnp.concatenate([gate_grad, gate_swap], -1)
    up_all = jnp.concatenate([up_grad, up_swap], -1)
    grad_part = (
        jnp.einsum("semf,edf->semd", gate_all, gate_mine, preferred_element_type=jnp.float32)
        + jnp.einsum("semf,edf->semd", up_all, up_mine, preferred_element_type=jnp.float32)
    ).astype(jnp.bfloat16)

    back_out = lax.all_to_all(out_rows, "expert", split_axis=0, concat_axis=0, tiled=True)
    picked = back_out.reshape(-1, model_width)[jnp.maximum(fwd_local, 0)].reshape(-1, choices_per, model_width)
    weights = jnp.where(fwd_mine, mixing.reshape(-1), 0.0).reshape(-1, choices_per)
    partial = jnp.sum(weights[:, :, None] * picked.astype(jnp.float32), 1)
    partial_other = swapped(partial)
    first = side == 0
    layer_out = (
        (inputs.astype(jnp.float32) + jnp.where(first, partial, partial_other))
        + jnp.where(first, partial_other, partial)
    ).astype(jnp.bfloat16)
    next_fwd = passed_along(layer_out, "section", 1)[None]

    back_grad = lax.all_to_all(grad_part, "expert", split_axis=0, concat_axis=0, tiled=True)
    grad_in_part = lax.dynamic_slice_in_dim(grad_in, mine, half, 1)
    input_grad = mix_rows(grad_in_part, back_grad, back_positions, unit_weights, choices_per)
    next_bwd = handoff(input_grad, -1)[None]
    gate_sum = gate_term.astype(jnp.bfloat16)
    up_sum = up_term.astype(jnp.bfloat16)
    down_sum = down_term.astype(jnp.bfloat16)
    return (next_fwd, next_bwd, gate_sum[None], up_sum[None], down_sum[None])


def solution(mesh):
    in_specs = (
        P("section", "expert", None),
        P("section", "expert", None),
        P("section", "expert", None),
        P("section", "expert", None),
        P("section", "expert", None),
        P("section", "expert", None),
        P("section", "expert", None),
        P("section", "expert", None, "dp"),
        P("section", "expert", None, "dp"),
        P("section", "expert", "dp", None),
    )
    out_specs = (
        P("section", "expert", None),
        P("section", "expert", None),
        P("section", "expert", None, "dp"),
        P("section", "expert", None, "dp"),
        P("section", "expert", "dp", None),
    )
    return jax.shard_map(local, mesh=mesh, in_specs=in_specs, out_specs=out_specs, check_vma=False)
```

```python
import functools

import jax
import jax.numpy as jnp
from jax import lax
from jax.experimental import pallas as pl
from jax.experimental.pallas import tpu as pltpu
from jax.sharding import PartitionSpec as P

MESH = pl.DeviceIdType.MESH

EXPERTS = 32
MOST = 26


def passed_along(block, axis, distance):
    devices = range(lax.axis_size(axis))
    route = [((i - distance) % len(devices), i) for i in devices]
    return lax.ppermute(block, axis, route)


def swapped(block):
    return lax.ppermute(block, "dp", [(0, 1), (1, 0)])


def exchange_kernel(n, spread, swapped_count, *refs):
    sends = refs[0:spread]
    swaps_out = refs[spread:spread + swapped_count]
    recvs = refs[spread + swapped_count:2 * spread + swapped_count]
    swaps_in = refs[2 * spread + swapped_count:2 * (spread + swapped_count)]
    send_sems, recv_sems, w_send, w_recv, local_sems = refs[2 * (spread + swapped_count):]
    me = lax.axis_index("expert")
    other = 1 - lax.axis_index("dp")

    barrier = pltpu.get_barrier_semaphore()

    def greet(o, carry):
        pl.semaphore_signal(barrier, 1, device_id={"expert": lax.rem(me + o, n)}, device_id_type=MESH)
        return carry

    lax.fori_loop(1, n, greet, 0)
    if swapped_count:
        pl.semaphore_signal(barrier, 1, device_id={"dp": other}, device_id_type=MESH)
    pl.semaphore_wait(barrier, n if swapped_count else n - 1)

    def copy_of(a, o):
        target = lax.rem(me + o, n)
        return pltpu.make_async_remote_copy(
            src_ref=sends[a].at[target],
            dst_ref=recvs[a].at[me],
            send_sem=send_sems.at[a, o],
            recv_sem=recv_sems.at[a, o],
            device_id={"expert": target},
            device_id_type=MESH,
        )

    swaps = [
        pltpu.make_async_remote_copy(
            src_ref=swaps_out[i],
            dst_ref=swaps_in[i],
            send_sem=w_send.at[i],
            recv_sem=w_recv.at[i],
            device_id={"dp": other},
            device_id_type=MESH,
        )
        for i in range(swapped_count)
    ]
    for swap in swaps:
        swap.start()
    locals_ = [
        pltpu.make_async_copy(sends[a].at[me], recvs[a].at[me], local_sems.at[a]) for a in range(spread)
    ]
    for a in range(spread):
        locals_[a].start()

        def start(o, carry, a=a):
            copy_of(a, o).start()
            return carry

        lax.fori_loop(1, n, start, 0)
    for a in range(spread):

        def finish(o, carry, a=a):
            copy_of(a, o).wait()
            return carry

        lax.fori_loop(1, n, finish, 0)
        locals_[a].wait()
    for swap in swaps:
        swap.wait()


def exchange(sends, swaps_out, collective_id):
    n = sends[0].shape[0]
    anywhere = pl.BlockSpec(memory_space=pl.ANY)
    arrays = (*sends, *swaps_out)
    moved = sum(x.size * x.dtype.itemsize for x in arrays)
    outs = pl.pallas_call(
        functools.partial(exchange_kernel, n, len(sends), len(swaps_out)),
        out_shape=[jax.ShapeDtypeStruct(x.shape, x.dtype) for x in arrays],
        in_specs=[anywhere] * len(arrays),
        out_specs=[anywhere] * len(arrays),
        scratch_shapes=[
            pltpu.SemaphoreType.DMA((len(sends), n)),
            pltpu.SemaphoreType.DMA((len(sends), n)),
            pltpu.SemaphoreType.DMA((max(1, len(swaps_out)),)),
            pltpu.SemaphoreType.DMA((max(1, len(swaps_out)),)),
            pltpu.SemaphoreType.DMA((len(sends),)),
        ],
        compiler_params=pltpu.CompilerParams(collective_id=collective_id, has_side_effects=True),
        cost_estimate=pl.CostEstimate(flops=0, bytes_accessed=2 * moved, transcendentals=0),
    )(*arrays)
    return outs[: len(sends)], outs[len(sends):]


def slot_ranks(routes):
    flat_routes = routes.reshape(-1)
    onehot_table = (flat_routes[:, None] == jnp.arange(EXPERTS, dtype=jnp.int32)[None, :]).astype(
        jnp.int32
    )
    earlier = jnp.cumsum(onehot_table, 0) - onehot_table
    return (flat_routes, jnp.sum(earlier * onehot_table, 1))


def combine_weights(numerators):
    counted = numerators.astype(jnp.float32)
    return counted / jnp.sum(counted, -1, keepdims=True)


def slot_table(positions, choices_per, depth=MOST):
    slots = jnp.arange(EXPERTS * depth, dtype=jnp.int32)
    return slots[:, None, None] == positions.reshape(-1, choices_per)[None, :, :]


def packed_rows(rows, table, scale=None, depth=MOST):
    chosen = jnp.any(table, -1).reshape(EXPERTS, depth, -1)
    picked = jnp.einsum("ecm,md->ecd", chosen.astype(rows.dtype), rows, preferred_element_type=jnp.float32)
    if scale is not None:
        picked = picked * jnp.sum(jnp.where(table, scale[None], 0.0), (1, 2)).reshape(EXPERTS, depth, 1)
    return picked.astype(rows.dtype)


def handoff(value, direction):
    sections = lax.axis_size("section")
    same = passed_along(value, "section", direction)
    route = [(i * 2 + j, ((i + direction) % sections) * 2 + 1 - j) for i in range(sections) for j in range(2)]
    crossed = lax.ppermute(value, ("section", "dp"), route)
    first = lax.axis_index("dp") == 0
    return jnp.concatenate([jnp.where(first, same, crossed), jnp.where(first, crossed, same)], 1)


def project(rows, gate_weight, up_weight):
    gate_value = jnp.einsum("semd,edf->semf", rows, gate_weight, preferred_element_type=jnp.float32)
    up_value = jnp.einsum("semd,edf->semf", rows, up_weight, preferred_element_type=jnp.float32)
    return (gate_value, up_value)


def local_backward(gate_value, up_value, grad_rows, down_weight):
    silu_gate = jax.nn.silu(gate_value)
    sigmoid_gate = jax.nn.sigmoid(gate_value)
    hidden = (silu_gate * up_value).astype(jnp.bfloat16)
    hidden_grad = jnp.einsum(
        "semd,efd->semf", grad_rows, down_weight, preferred_element_type=jnp.float32
    )
    up_grad = (hidden_grad * silu_gate).astype(jnp.bfloat16)
    gate_grad = (
        hidden_grad * up_value * sigmoid_gate * (1.0 + gate_value * (1.0 - sigmoid_gate))
    ).astype(jnp.bfloat16)
    return (hidden, gate_grad, up_grad)


def weight_terms(saved_rows, grad_rows, back_hidden, gate_grad, up_grad):
    gate_term = jnp.einsum(
        "semd,semf->edf", saved_rows, gate_grad, preferred_element_type=jnp.float32
    )
    up_term = jnp.einsum("semd,semf->edf", saved_rows, up_grad, preferred_element_type=jnp.float32)
    down_term = jnp.einsum(
        "semf,semd->efd", back_hidden, grad_rows, preferred_element_type=jnp.float32
    )
    return (gate_term, up_term, down_term)


def mix_rows(base, returned, positions, weights, choices_per):
    width = returned.shape[-1]
    picked = (
        returned.reshape(-1, width)[positions].reshape(-1, choices_per, width).astype(jnp.float32)
    )
    return (base.astype(jnp.float32) + jnp.sum(weights[:, :, None] * picked, 1)).astype(
        jnp.bfloat16
    )


def local(
    fwd_in, fwd_routes, fwd_numer, bwd_saved, bwd_routes, bwd_numer, bwd_grad, w_gate, w_up, w_down
):
    groups = lax.axis_size("expert")
    inputs = fwd_in[0]
    saved = bwd_saved[0]
    grad_in = bwd_grad[0]
    model_width = inputs.shape[-1]
    half = model_width // lax.axis_size("dp")
    mine = lax.axis_index("dp") * half
    theirs = half - mine
    choices_per = fwd_routes.shape[-1]
    gate_half = w_gate[0]
    up_half = w_up[0]
    down_half = w_down[0]

    fwd_flat, fwd_rank = slot_ranks(fwd_routes[0])
    back_flat, back_rank = slot_ranks(bwd_routes[0])
    back_positions = back_flat * MOST + back_rank
    mixing = combine_weights(fwd_numer[0])
    back_mixing = combine_weights(bwd_numer[0])
    unit_weights = jnp.ones_like(back_mixing)
    back_table = slot_table(back_positions, choices_per)
    send_saved = packed_rows(saved, back_table)
    send_grad = packed_rows(grad_in, back_table, back_mixing)
    (recv_saved, recv_grad), (gate_other, up_other, down_other) = exchange(
        (send_saved, send_grad), (gate_half[0], up_half[0], down_half[0]), 0
    )
    recv_saved, recv_grad = (x.reshape(groups, 1, MOST, model_width) for x in (recv_saved, recv_grad))
    gate_full = jnp.concatenate([gate_half[0], gate_other], 1)
    up_full = jnp.concatenate([up_half[0], up_other], 1)
    down_full = jnp.concatenate([down_half[0], down_other], 0)
    gate_mine = lax.dynamic_slice_in_dim(gate_full, mine, half, 0)[None]
    up_mine = lax.dynamic_slice_in_dim(up_full, mine, half, 0)[None]

    share = MOST // 2
    side = lax.axis_index("dp")
    fwd_mine = (fwd_rank >= share).astype(jnp.int32) == side
    fwd_local = jnp.where(fwd_mine, fwd_flat * share + fwd_rank - side * share, -1)
    fwd_table = slot_table(fwd_local, choices_per, share)
    send_inputs = packed_rows(inputs, fwd_table, depth=share)
    recv_inputs = lax.all_to_all(send_inputs, "expert", split_axis=0, concat_axis=0, tiled=True)
    gate_value = jnp.einsum("smd,df->smf", recv_inputs, gate_full, preferred_element_type=jnp.float32)
    up_value = jnp.einsum("smd,df->smf", recv_inputs, up_full, preferred_element_type=jnp.float32)
    hidden = (jax.nn.silu(gate_value) * up_value).astype(jnp.bfloat16)
    out_rows = jnp.einsum(
        "smf,fd->smd", hidden, down_full, preferred_element_type=jnp.float32
    ).astype(jnp.bfloat16)

    out_rows, recv_saved, recv_grad = lax.optimization_barrier((out_rows, recv_saved, recv_grad))
    back_gate, back_up = project(recv_saved, gate_half, up_half)
    back_hidden, gate_grad, up_grad = local_backward(back_gate, back_up, recv_grad, down_half)
    gate_term, up_term, down_term = weight_terms(
        recv_saved, recv_grad, back_hidden, gate_grad, up_grad
    )
    gate_swap, up_swap = swapped((gate_grad, up_grad))
    gate_all = jnp.concatenate([gate_grad, gate_swap], -1)
    up_all = jnp.concatenate([up_grad, up_swap], -1)
    grad_part = (
        jnp.einsum("semf,edf->semd", gate_all, gate_mine, preferred_element_type=jnp.float32)
        + jnp.einsum("semf,edf->semd", up_all, up_mine, preferred_element_type=jnp.float32)
    ).astype(jnp.bfloat16)

    back_out = lax.all_to_all(out_rows, "expert", split_axis=0, concat_axis=0, tiled=True)
    picked = back_out.reshape(-1, model_width)[jnp.maximum(fwd_local, 0)].reshape(-1, choices_per, model_width)
    weights = jnp.where(fwd_mine, mixing.reshape(-1), 0.0).reshape(-1, choices_per)
    partial = jnp.sum(weights[:, :, None] * picked.astype(jnp.float32), 1)
    partial_other = swapped(partial)
    first = side == 0
    layer_out = (
        (inputs.astype(jnp.float32) + jnp.where(first, partial, partial_other))
        + jnp.where(first, partial_other, partial)
    ).astype(jnp.bfloat16)
    next_fwd = passed_along(layer_out, "section", 1)[None]

    back_grad = lax.all_to_all(grad_part, "expert", split_axis=0, concat_axis=0, tiled=True)
    grad_in_part = lax.dynamic_slice_in_dim(grad_in, mine, half, 1)
    input_grad = mix_rows(grad_in_part, back_grad, back_positions, unit_weights, choices_per)
    next_bwd = handoff(input_grad, -1)[None]
    gate_sum = gate_term.astype(jnp.bfloat16)
    up_sum = up_term.astype(jnp.bfloat16)
    down_sum = down_term.astype(jnp.bfloat16)
    return (next_fwd, next_bwd, gate_sum[None], up_sum[None], down_sum[None])


def solution(mesh):
    in_specs = (
        P("section", "expert", None),
        P("section", "expert", None),
        P("section", "expert", None),
        P("section", "expert", None),
        P("section", "expert", None),
        P("section", "expert", None),
        P("section", "expert", None),
        P("section", "expert", None, "dp"),
        P("section", "expert", None, "dp"),
        P("section", "expert", "dp", None),
    )
    out_specs = (
        P("section", "expert", None),
        P("section", "expert", None),
        P("section", "expert", None, "dp"),
        P("section", "expert", None, "dp"),
        P("section", "expert", "dp", None),
    )
    return jax.shard_map(local, mesh=mesh, in_specs=in_specs, out_specs=out_specs, check_vma=False)
```
